32 devices in a mesh: gx: 4 (over x, core), gy: 8 (over z, y).
Axes of the slice: x: 2, y: 2, z: 4, core: 2. Of those that a mesh axis runs over, the one named last changes fastest.
Arguments:
- first_image: float32 [32, 64, 128], P('gx', 'gy'), may hold values from -6 to 6
- second_image: float32 [32, 64, 128], P('gx', 'gy'), may hold values from -6 to 6
- start_flow: float32 [3, 32, 64, 128], P(None, 'gx', 'gy'), may hold values from -3 to 3
Outputs:
- flow: float32 [3, 32, 64, 128], P(None, 'gx', 'gy')
The draws below stay inside these ranges and needn't reach their ends.
All inputs are finite; a program needn't handle non-finite values.
Results may differ from the reference program's by a relative error of at most 0.0001.
Values sent between devices are 32-bit elements; how exact they have to be, the bound alone decides.
A program may use at most 128 MiB of HBM per device.

```python
import jax
import jax.numpy as jnp
from jax import lax

SWEEPS = 4
COARSE_SWEEPS = 12
CYCLES = 2
NX = 32
NY = 64
NZ = 128


def steps_of(rng, extent, split, smallest, high):
    level = 1.0
    for position, parts in split:
        draws = jax.random.uniform(jax.random.fold_in(jax.random.fold_in(rng, 6), position), (parts,), jnp.float32, smallest / len(split), high / len(split))
        level = level * jnp.repeat(jnp.exp(draws), extent[position] // parts).reshape((-1,) + (1,) * (len(extent) - 1 - position))
    return level


def bell_draw(stream_key, dims, scale, reach, cuts=(), kind=jnp.bfloat16):
    gain = steps_of(stream_key, dims, cuts, -0.22, 0.18) if cuts else 1.0
    drawn = jax.random.normal(stream_key, dims, jnp.float32) * scale * gain
    return jnp.minimum(jnp.maximum(drawn, -reach), reach).astype(kind)


def setup_inputs(seed: int = 0) -> dict:
    splits = jax.random.split(jax.random.key(seed), 4)
    return {
        "first_image": bell_draw(splits[0], (NX, NY, NZ), 1.0, 6.0, ((0, 4), (1, 8)), jnp.float32),
        "second_image": bell_draw(splits[1], (NX, NY, NZ), 1.0, 6.0, ((0, 4), (1, 8)), jnp.float32),
        "start_flow": bell_draw(splits[2], (3, NX, NY, NZ), 0.5, 3.0, ((1, 4), (2, 8)), jnp.float32),
    }


damping = 0.6
smooth_weight = 2.0
edge_scale = 0.25
floor_grad = 0.5

def pad_cells(field):
    widths = [(0, 0)] * (field.ndim - 3) + [(1, 1)] * 3
    return jnp.pad(field, widths)

def neighbours(padded):
    return [padded[..., 2:, 1:-1, 1:-1], padded[..., :-2, 1:-1, 1:-1], padded[..., 1:-1, 2:, 1:-1], padded[..., 1:-1, :-2, 1:-1], padded[..., 1:-1, 1:-1, 2:], padded[..., 1:-1, 1:-1, :-2]]

def centre(padded):
    return padded[..., 1:-1, 1:-1, 1:-1]

def diffusivity(padded_flow):
    beside_all = neighbours(padded_flow)
    total = jnp.zeros(centre(padded_flow).shape[1:], padded_flow.dtype)
    for upper, lower in ((0, 1), (2, 3), (4, 5)):
        slope = 0.5 * (beside_all[upper] - beside_all[lower])
        total = total + lax.optimization_barrier(jnp.sum(slope * slope, axis=0))
    return lax.rsqrt(1.0 + total / edge_scale)

def motion_tensor(padded_images):
    mean_image = 0.5 * (padded_images[0] + padded_images[1])
    beside_all = neighbours(mean_image)
    slopes = [0.5 * (beside_all[0] - beside_all[1]), 0.5 * (beside_all[2] - beside_all[3]), 0.5 * (beside_all[4] - beside_all[5])]
    change = centre(padded_images[1]) - centre(padded_images[0])
    scale = 1.0 / (slopes[0] * slopes[0] + slopes[1] * slopes[1] + slopes[2] * slopes[2] + floor_grad)
    tensor = jnp.stack([scale * slopes[0] * slopes[0], scale * slopes[0] * slopes[1], scale * slopes[0] * slopes[2], scale * slopes[1] * slopes[1], scale * slopes[1] * slopes[2], scale * slopes[2] * slopes[2]])
    source = jnp.stack([-scale * slopes[0] * change, -scale * slopes[1] * change, -scale * slopes[2] * change])
    return (tensor, source)

def apply_sym(matrix, vector):
    first = matrix[0] * vector[0] + matrix[1] * vector[1] + matrix[2] * vector[2]
    second = matrix[1] * vector[0] + matrix[3] * vector[1] + matrix[4] * vector[2]
    third = matrix[2] * vector[0] + matrix[4] * vector[1] + matrix[5] * vector[2]
    return jnp.stack([first, second, third])

def inverse_sym(tensor, total):
    aaa = tensor[0] + total
    bbb = tensor[1]
    ccc = tensor[2]
    ddd = tensor[3] + total
    eee = tensor[4]
    fff = tensor[5] + total
    cof_a = ddd * fff - eee * eee
    cof_b = ccc * eee - bbb * fff
    cof_c = bbb * eee - ccc * ddd
    cof_d = aaa * fff - ccc * ccc
    cof_e = bbb * ccc - aaa * eee
    cof_f = aaa * ddd - bbb * bbb
    determinant = aaa * cof_a + bbb * cof_b + ccc * cof_c
    return jnp.stack([cof_a, cof_b, cof_c, cof_d, cof_e, cof_f]) / determinant

def prepare(tensor, padded_weight, scale):
    middle = centre(padded_weight)
    faces = [scale * 2.0 * middle * other / (middle + other) for other in neighbours(padded_weight)]
    total = faces[0] + faces[1] + faces[2] + faces[3] + faces[4] + faces[5]
    return (tensor, jnp.stack(faces), total, inverse_sym(tensor, total))

def inflow(padded_field, level):
    faces = level[1]
    beside_all = neighbours(padded_field)
    result = faces[0] * beside_all[0]
    for index in range(1, 6):
        result = result + faces[index] * beside_all[index]
    return result

def relaxed(field, padded_field, source, level):
    return (1.0 - damping) * field + damping * apply_sym(level[3], source + inflow(padded_field, level))

def residual(field, padded_field, source, level):
    return source + inflow(padded_field, level) - apply_sym(level[0], field) - level[2] * field

def restrict(field, ratio):
    front = field.shape[:-3]
    across, along, depth = field.shape[-3:]
    blocks = field.reshape(front + (across // ratio, ratio, along // ratio, ratio, depth // ratio, ratio))
    return lax.optimization_barrier(jnp.mean(blocks, axis=(-5, -3, -1)))

def refine(padded, axis, ratio):
    count = padded.shape[axis] - 2
    middle = lax.slice_in_dim(padded, 1, count + 1, axis=axis)
    below = lax.slice_in_dim(padded, 0, count, axis=axis)
    above = lax.slice_in_dim(padded, 2, count + 2, axis=axis)
    pieces = []
    for offset in range(ratio):
        shift = (offset + 0.5) / ratio - 0.5
        other = below if shift < 0 else above
        pieces.append((1.0 - abs(shift)) * middle + abs(shift) * other)
    stacked = jnp.stack(pieces, axis=axis + 1)
    shape = list(middle.shape)
    shape[axis] = count * ratio
    return stacked.reshape(shape)

def refine_cells(padded, ratio):
    for axis in (1, 2, 3):
        padded = refine(padded, axis, ratio)
    return padded

def reference(first_image, second_image, start_flow):
    tensor, source = motion_tensor(pad_cells(jnp.stack([first_image, second_image])))
    mid_tensor = restrict(tensor, 2)
    coarse_tensor = restrict(mid_tensor, 4)
    flow = start_flow
    for cycle in range(CYCLES):
        weight = diffusivity(pad_cells(flow))
        fine = prepare(tensor, pad_cells(weight), smooth_weight)
        for sweep in range(SWEEPS):
            flow = relaxed(flow, pad_cells(flow), source, fine)
        fine_rest = residual(flow, pad_cells(flow), source, fine)
        mid_weight = restrict(weight, 2)
        mid = prepare(mid_tensor, pad_cells(mid_weight), smooth_weight / 4.0)
        mid_source = restrict(fine_rest, 2)
        error = damping * apply_sym(mid[3], mid_source)
        for sweep in range(SWEEPS - 1):
            error = relaxed(error, pad_cells(error), mid_source, mid)
        mid_rest = residual(error, pad_cells(error), mid_source, mid)
        unit_weight = jnp.ones(coarse_tensor.shape[1:], coarse_tensor.dtype)
        coarse = prepare(coarse_tensor, pad_cells(unit_weight), smooth_weight / 64.0)
        coarse_source = restrict(mid_rest, 4)
        correction = damping * apply_sym(coarse[3], coarse_source)

        def coarse_turn(index, current):
            return relaxed(current, pad_cells(current), coarse_source, coarse)
        correction = lax.fori_loop(0, COARSE_SWEEPS - 1, coarse_turn, correction)
        error = error + refine_cells(pad_cells(correction), 4)
        for sweep in range(SWEEPS):
            error = relaxed(error, pad_cells(error), mid_source, mid)
        flow = flow + refine_cells(pad_cells(error), 2)
        for sweep in range(SWEEPS):
            flow = relaxed(flow, pad_cells(flow), source, fine)
    return flow
```

```python
import functools

import jax
import jax.numpy as jnp
from jax import lax
from jax.experimental import pallas as pl
from jax.experimental.pallas import tpu as pltpu
from jax.sharding import PartitionSpec as P

SWEEPS = 4
COARSE_SWEEPS = 12
CYCLES = 2
damping = 0.6
smooth_weight = 2.0
edge_scale = 0.25
floor_grad = 0.5
TINY = 1e-30

MESH = pl.DeviceIdType.MESH
SIDES = ((-1, 0), (1, 0), (0, -1), (0, 1))
AROUND = tuple((i, j) for i in (-1, 0, 1) for j in (-1, 0, 1) if (i, j) != (0, 0))
FINE_ROUNDS = 2 + 2 * SWEEPS
BLOCK_ROUNDS = 4


def sym(m, v):
    return [
        m[0] * v[0] + m[1] * v[1] + m[2] * v[2],
        m[1] * v[0] + m[3] * v[1] + m[4] * v[2],
        m[2] * v[0] + m[4] * v[1] + m[5] * v[2],
    ]


def damped_inverse(t, total):
    a, b, c, d, e, f = t[0] + total, t[1], t[2], t[3] + total, t[4], t[5] + total
    cof = [
        d * f - e * e,
        c * e - b * f,
        b * e - c * d,
        a * f - c * c,
        b * c - a * e,
        a * d - b * b,
    ]
    det = a * cof[0] + b * cof[1] + c * cof[2]
    factor = damping / jnp.where(total > 0.0, det, 1.0)
    return [factor * value for value in cof]


def kernel(
    GX, GY, NR, first_ref, second_ref, start_ref, flow_ref,
    mean_ref, weight_ref, tensor_ref, source_ref, face_ref, inv_ref,
    mid_t, mid_w, mid_face, mid_inv, mid_src, err,
    coarse_inv, coarse_src, corr,
    xh, yh, ys, bs, br, gs, gb,
    f_send, f_recv, b_send, b_recv, g_send, g_recv,
):
    gx = lax.axis_index("gx")
    gy = lax.axis_index("gy")
    me = gx * GY + gy
    n = GX * GY
    GT = GY // 8
    NM = NR // 2
    WR = 3 * NM
    shape = (8, 128)
    lane = lax.broadcasted_iota(jnp.int32, shape, 1)
    sub = lax.broadcasted_iota(jnp.int32, shape, 0)
    zero = jnp.zeros(shape, jnp.float32)

    def lroll(v, k):
        return pltpu.roll(v, k % 128, 1)

    def sroll(v, k):
        return pltpu.roll(v, k % 8, 0)

    def lane_bit(k):
        return (lane & k) == 0

    def sub_bit(k):
        return (sub & k) == 0

    def lane_pair(v, k):
        return v + jnp.where(lane_bit(k), lroll(v, -k), lroll(v, k))

    def sub_pair(v, k):
        return v + jnp.where(sub_bit(k), sroll(v, -k), sroll(v, k))

    def zup(v, k):
        return jnp.where(lane < 128 - k, lroll(v, -k), 0.0)

    def zdn(v, k):
        return jnp.where(lane >= k, lroll(v, k), 0.0)

    def y_shifts(tiles, k):
        count = len(tiles)
        ups = [sroll(v, -k) for v in tiles] + [zero]
        downs = [zero] + [sroll(v, k) for v in tiles]
        return (
            [jnp.where(sub < 8 - k, ups[j], ups[j + 1]) for j in range(count)],
            [jnp.where(sub >= k, downs[j + 1], downs[j]) for j in range(count)],
        )

    def here(dx, dy):
        conds = []
        if dx:
            conds.append((gx + dx >= 0) & (gx + dx < GX))
        if dy:
            conds.append((gy + dy >= 0) & (gy + dy < GY))
        return functools.reduce(lambda p, q: p & q, conds)

    for ref in (xh, yh, br, corr):
        flat = 1
        for extent in ref.shape[:-2]:
            flat *= extent
        ref[...] = jnp.zeros(ref.shape, jnp.float32)

    barrier = pltpu.get_barrier_semaphore()

    def greet(d, carry):
        other = lax.rem(me + d, n)
        pl.semaphore_signal(
            barrier, inc=1, device_id=(other // GY, lax.rem(other, GY)), device_id_type=MESH
        )
        return carry

    lax.fori_loop(1, n, greet, 0)
    pl.semaphore_wait(barrier, n - 1)

    def side_copy(ref, count, slot, k):
        dx, dy = SIDES[k]
        back = k ^ 1
        if dx:
            src = ref.at[pl.ds(0, count), 0 if dx < 0 else NR - 1]
            dst = xh.at[slot, back, pl.ds(0, count)]
        else:
            src = ys.at[slot, k - 2, pl.ds(0, count)]
            dst = yh.at[slot, back - 2, pl.ds(0, count)]
        return pltpu.make_async_remote_copy(
            src_ref=src, dst_ref=dst,
            send_sem=f_send.at[slot, k], recv_sem=f_recv.at[slot, back],
            device_id=(gx + dx, gy + dy), device_id_type=MESH,
        )

    def side_arrival(ref, count, slot, k):
        dx, dy = SIDES[k]
        if dx:
            dst = xh.at[slot, k, pl.ds(0, count)]
        else:
            dst = yh.at[slot, k - 2, pl.ds(0, count)]
        return pltpu.make_async_remote_copy(
            src_ref=dst, dst_ref=dst,
            send_sem=f_send.at[slot, k], recv_sem=f_recv.at[slot, k],
            device_id=(gx + dx, gy + dy), device_id_type=MESH,
        )

    def fine_start(ref, count, slot):
        for c in range(count):
            ys[slot, 0, c] = ref[c, :, 0, :]
            ys[slot, 1, c] = ref[c, :, 7, :]
        for k in (2, 3, 0, 1):
            @pl.when(here(*SIDES[k]))
            def _(k=k):
                side_copy(ref, count, slot, k).start()

    def fine_wait(ref, count, slot):
        for k in (0, 1, 2, 3):
            @pl.when(here(*SIDES[k]))
            def _(k=k):
                side_arrival(ref, count, slot, k).wait_recv()
                side_copy(ref, count, slot, k).wait_send()

    def block_copy(count, slot, k):
        dx, dy = AROUND[k]
        return pltpu.make_async_remote_copy(
            src_ref=bs.at[slot, pl.ds(0, count)],
            dst_ref=br.at[slot, 7 - k, pl.ds(0, count)],
            send_sem=b_send.at[slot, k], recv_sem=b_recv.at[slot, 7 - k],
            device_id=(gx + dx, gy + dy), device_id_type=MESH,
        )

    def block_arrival(count, slot, k):
        dx, dy = AROUND[k]
        dst = br.at[slot, k, pl.ds(0, count)]
        return pltpu.make_async_remote_copy(
            src_ref=dst, dst_ref=dst,
            send_sem=b_send.at[slot, k], recv_sem=b_recv.at[slot, k],
            device_id=(gx + dx, gy + dy), device_id_type=MESH,
        )

    def pack(rows):
        lower = jnp.where(lane_bit(1), rows[0], rows[1])
        upper = jnp.where(lane_bit(1), rows[2], rows[3])
        return jnp.where(sub_bit(1), lower, upper)

    def unpack(v):
        even = jnp.where(lane_bit(1), v, lroll(v, 1))
        odd = jnp.where(lane_bit(1), lroll(v, -1), v)

        def split(w):
            return (
                jnp.where(sub_bit(1), w, sroll(w, 1)),
                jnp.where(sub_bit(1), sroll(w, -1), w),
            )

        e, o = split(even), split(odd)
        return [e[0], o[0], e[1], o[1]]

    def block_start(fields, slot):
        for i, rows in enumerate(fields):
            bs[slot, i] = pack(rows)
        for k in range(8):
            @pl.when(here(*AROUND[k]))
            def _(k=k):
                block_copy(len(fields), slot, k).start()

    def block_wait(count, slot):
        for k in range(8):
            @pl.when(here(*AROUND[k]))
            def _(k=k):
                block_arrival(count, slot, k).wait_recv()
                block_copy(count, slot, k).wait_send()

    def block_spread(places, slot):
        for k, (dx, dy) in enumerate(AROUND):
            for i, place in enumerate(places):
                for r, v in enumerate(unpack(br[slot, k, i])):
                    place[NM * (dx + 1) + r, dy + 1] = v

    def keep_own(place, rows):
        for r, v in enumerate(rows):
            place[NM + r, 1] = v

    def gather_copy(slot, other):
        return pltpu.make_async_remote_copy(
            src_ref=gs.at[slot], dst_ref=gb.at[slot, me],
            send_sem=g_send.at[slot], recv_sem=g_recv.at[slot],
            device_id=(other // GY, lax.rem(other, GY)), device_id_type=MESH,
        )

    def gather_start(values, slot):
        row = zero
        for i, v in enumerate(values):
            row = jnp.where((lane & 7) == i, v, row)
        gs[slot] = row[0:1]
        gb[slot, me] = row[0:1]

        def send(d, carry):
            gather_copy(slot, lax.rem(me + d, n)).start()
            return carry

        lax.fori_loop(1, n, send, 0)

    def gather_wait(slot):
        whole = gb.at[slot, pl.ds(0, n - 1)]
        copy = pltpu.make_async_remote_copy(
            src_ref=whole, dst_ref=whole,
            send_sem=g_send.at[slot], recv_sem=g_recv.at[slot],
            device_id=(gx, gy), device_id_type=MESH,
        )
        copy.wait_recv()
        copy.wait_send()

    def gathered(slot, count, g, t):
        packed = gb[slot, pl.ds(g * GY + t * 8, 8), 0, :]
        result = []
        for i in range(count):
            v = jnp.where((lane & 7) == i, packed, 0.0)
            for k in (1, 2, 4):
                v = lane_pair(v, k)
            result.append(v)
        return result

    def restrict_fine(rows):
        result = []
        for m in range(NM):
            v = rows[2 * m] + rows[2 * m + 1]
            result.append(sub_pair(lane_pair(v, 1), 1) * 0.125)
        return result

    def restrict_mid(rows):
        v = functools.reduce(lambda p, q: p + q, rows)
        for k in (2, 4):
            v = lane_pair(v, k)
            v = sub_pair(v, k)
        return v * (1.0 / 64.0)

    def fine_rows(ref, c, slot):
        return [xh[slot, 0, c]] + [ref[c, x] for x in range(NR)] + [xh[slot, 1, c]]

    def fine_y(rows, c, slot, x):
        v = rows[x + 1]
        up = jnp.where(sub < 7, sroll(v, -1), yh[slot, 1, c, x:x + 1, :])
        down = jnp.where(sub >= 1, sroll(v, 1), yh[slot, 0, c, x:x + 1, :])
        return up, down

    for x in range(NR):
        mean_ref[0, x] = 0.5 * (first_ref[x] + second_ref[x])
        for c in range(3):
            flow_ref[c, x] = start_ref[c, x]
    fine_start(mean_ref, 1, 0)
    fine_wait(mean_ref, 1, 0)
    rows = fine_rows(mean_ref, 0, 0)
    for x in range(NR):
        up, down = fine_y(rows, 0, 0, x)
        s0 = 0.5 * (rows[x + 2] - rows[x])
        s1 = 0.5 * (up - down)
        s2 = 0.5 * (zup(rows[x + 1], 1) - zdn(rows[x + 1], 1))
        change = second_ref[x] - first_ref[x]
        scale = 1.0 / (s0 * s0 + s1 * s1 + s2 * s2 + floor_grad)
        a0, a1, a2 = scale * s0, scale * s1, scale * s2
        for i, v in enumerate((a0 * s0, a0 * s1, a0 * s2, a1 * s1, a1 * s2, a2 * s2)):
            tensor_ref[i, x] = v
        for i, v in enumerate((a0, a1, a2)):
            source_ref[i, x] = -v * change
    mids, coarses = [], []
    for i in range(6):
        own = restrict_fine([tensor_ref[i, x] for x in range(NR)])
        keep_own(mid_t.at[i], own)
        mids.append(own)
        coarses.append(restrict_mid(own))
    block_start(mids, 0)
    gather_start(coarses, 0)
    block_wait(6, 0)
    block_spread([mid_t.at[i] for i in range(6)], 0)
    gather_wait(0)
    cface = smooth_weight / 64.0
    for g in range(GX):
        for t in range(GT):
            tensor = gathered(0, 6, g, t)
            count = jnp.where(lane < 120, 1.0, 0.0) + jnp.where(lane >= 8, 1.0, 0.0)
            count = count + jnp.where(sub + t * 8 < GY - 1, 1.0, 0.0)
            count = count + jnp.where(sub + t * 8 >= 1, 1.0, 0.0)
            count = count + float((g > 0) + (g < GX - 1))
            for i, v in enumerate(damped_inverse(tensor, cface * count)):
                coarse_inv[i, g, t] = v

    def fine_inflow(x, all_rows, slot):
        flows = []
        face = [face_ref[i, x] for i in range(6)]
        for c in range(3):
            rows = all_rows[c]
            up, down = fine_y(rows, c, slot, x)
            v = source_ref[c, x] + face[0] * rows[x + 2] + face[1] * rows[x]
            v = v + face[2] * up + face[3] * down
            v = v + face[4] * lroll(rows[x + 1], -1) + face[5] * lroll(rows[x + 1], 1)
            flows.append(v)
        return flows, face

    def fine_relax(slot):
        all_rows = [fine_rows(flow_ref, c, slot) for c in range(3)]
        for x in range(NR):
            flows, _ = fine_inflow(x, all_rows, slot)
            out = sym([inv_ref[i, x] for i in range(6)], flows)
            for c in range(3):
                flow_ref[c, x] = (1.0 - damping) * all_rows[c][x + 1] + out[c]

    def mid_inflow(r, p, tiles, wanted):
        flows = [[None] * 3 for _ in range(3)]
        for c in range(3):
            now = [err[p, c, r, j] for j in range(3)]
            tiles[c] = now
            ups, downs = y_shifts(now, 2)
            for j in wanted:
                v = mid_src[c, r, j] + mid_face[0, r, j] * err[p, c, r + 1, j]
                v = v + mid_face[1, r, j] * err[p, c, r - 1, j]
                v = v + mid_face[2, r, j] * ups[j] + mid_face[3, r, j] * downs[j]
                v = v + mid_face[4, r, j] * lroll(now[j], -2)
                flows[c][j] = v + mid_face[5, r, j] * lroll(now[j], 2)
        return flows

    def mid_relax(p, low):
        def turn(r, carry):
            tiles = [None] * 3
            flows = mid_inflow(r, p, tiles, (0, 1, 2))
            for j in range(3):
                out = sym([mid_inv[i, r, j] for i in range(6)], [flows[c][j] for c in range(3)])
                for c in range(3):
                    err[1 - p, c, r, j] = (1.0 - damping) * tiles[c][j] + out[c]
            return carry

        lax.fori_loop(low, WR - low, turn, 0)

    def mid_prepare():
        scale = 2.0 * smooth_weight / 4.0

        def turn(r, carry):
            now = [mid_w[r, j] for j in range(3)]
            has_up = jnp.where(r < WR - 1, 1.0, 0.0)
            has_down = jnp.where(r > 0, 1.0, 0.0)
            above = jnp.minimum(r + 1, WR - 1)
            below = jnp.maximum(r - 1, 0)
            ups, downs = y_shifts(now, 2)
            for j in range(3):
                v = now[j]
                beside = [
                    mid_w[above, j] * has_up, mid_w[below, j] * has_down,
                    ups[j], downs[j], zup(v, 2), zdn(v, 2),
                ]
                face = [scale * v * o / jnp.maximum(v + o, TINY) for o in beside]
                total = functools.reduce(lambda p, q: p + q, face)
                for i in range(6):
                    mid_face[i, r, j] = face[i]
                tensor = [mid_t[i, r, j] for i in range(6)]
                for i, w in enumerate(damped_inverse(tensor, total)):
                    mid_inv[i, r, j] = w
            return carry

        lax.fori_loop(0, WR, turn, 0)

    def cycle(cyc, carry):
        base = 1 + cyc * FINE_ROUNDS
        bbase = 1 + cyc * BLOCK_ROUNDS
        fine_start(flow_ref, 3, base)
        fine_wait(flow_ref, 3, base)
        q = [zero] * NR
        for c in range(3):
            rows = fine_rows(flow_ref, c, base)
            for x in range(NR):
                up, down = fine_y(rows, c, base, x)
                s0 = 0.5 * (rows[x + 2] - rows[x])
                s1 = 0.5 * (up - down)
                s2 = 0.5 * (zup(rows[x + 1], 1) - zdn(rows[x + 1], 1))
                q[x] = q[x] + s0 * s0 + s1 * s1 + s2 * s2
        weights = [lax.rsqrt(1.0 + v * (1.0 / edge_scale)) for v in q]
        for x in range(NR):
            weight_ref[0, x] = weights[x]
        fine_start(weight_ref, 1, base + 1)
        own_w = restrict_fine(weights)
        keep_own(mid_w, own_w)
        block_start([own_w], bbase)
        fine_wait(weight_ref, 1, base + 1)
        rows = fine_rows(weight_ref, 0, base + 1)
        for x in range(NR):
            v = rows[x + 1]
            up, down = fine_y(rows, 0, base + 1, x)
            beside = [rows[x + 2], rows[x], up, down, zup(v, 1), zdn(v, 1)]
            face = [2.0 * smooth_weight * v * o / (v + o) for o in beside]
            total = functools.reduce(lambda p, q: p + q, face)
            for i in range(6):
                face_ref[i, x] = face[i]
            tensor = [tensor_ref[i, x] for i in range(6)]
            for i, w in enumerate(damped_inverse(tensor, total)):
                inv_ref[i, x] = w
        fine_relax(base)
        for sweep in range(1, SWEEPS):
            slot = base + 1 + sweep
            fine_start(flow_ref, 3, slot)
            if sweep == 1:
                block_wait(1, bbase)
                block_spread([mid_w], bbase)
                mid_prepare()
            fine_wait(flow_ref, 3, slot)
            fine_relax(slot)
        slot = base + 1 + SWEEPS
        fine_start(flow_ref, 3, slot)
        fine_wait(flow_ref, 3, slot)
        all_rows = [fine_rows(flow_ref, c, slot) for c in range(3)]
        rest = [[], [], []]
        for x in range(NR):
            flows, face = fine_inflow(x, all_rows, slot)
            total = functools.reduce(lambda p, q: p + q, face)
            now = [all_rows[c][x + 1] for c in range(3)]
            out = sym([tensor_ref[i, x] for i in range(6)], now)
            for c in range(3):
                rest[c].append(flows[c] - out[c] - total * now[c])
        srcs = [restrict_fine(rest[c]) for c in range(3)]
        errs = [[], [], []]
        for r in range(NM):
            out = sym([mid_inv[i, NM + r, 1] for i in range(6)], [srcs[c][r] for c in range(3)])
            for c in range(3):
                errs[c].append(out[c])
        block_start(srcs + errs, bbase + 1)
        for c in range(3):
            keep_own(mid_src.at[c], srcs[c])
            keep_own(err.at[0, c], errs[c])
        block_wait(6, bbase + 1)
        block_spread([mid_src.at[c] for c in range(3)] + [err.at[0, c] for c in range(3)], bbase + 1)
        p = 0
        for sweep in range(1, SWEEPS):
            mid_relax(p, sweep)
            p = 1 - p
        mrest = [[], [], []]
        olds = [[], [], []]
        for r in range(NM, 2 * NM):
            tiles = [None] * 3
            flows = mid_inflow(r, p, tiles, (1,))
            total = functools.reduce(lambda a, b: a + b, [mid_face[i, r, 1] for i in range(6)])
            now = [tiles[c][1] for c in range(3)]
            out = sym([mid_t[i, r, 1] for i in range(6)], now)
            for c in range(3):
                mrest[c].append(flows[c][1] - out[c] - total * now[c])
                olds[c].append(now[c])
        gather_start([restrict_mid(mrest[c]) for c in range(3)], 1 + cyc)
        block_start(olds, bbase + 2)
        block_wait(3, bbase + 2)
        block_spread([err.at[p, c] for c in range(3)], bbase + 2)
        gather_wait(1 + cyc)

        current = []
        for g in range(GX):
            for t in range(GT):
                src = gathered(1 + cyc, 3, g, t)
                out = sym([coarse_inv[i, g, t] for i in range(6)], src)
                for c in range(3):
                    coarse_src[c, g, t] = src[c]
                current.append(out)

        def coarse_turn(index, now):
            result = []
            for g in range(GX):
                shifted = [
                    y_shifts([now[g * GT + t][c] for t in range(GT)], 1) for c in range(3)
                ]
                for t in range(GT):
                    flows = []
                    for c in range(3):
                        v = now[g * GT + t][c]
                        s = shifted[c][0][t] + shifted[c][1][t]
                        s = s + (zup(v, 8) + zdn(v, 8))
                        if g > 0:
                            s = s + now[(g - 1) * GT + t][c]
                        if g < GX - 1:
                            s = s + now[(g + 1) * GT + t][c]
                        flows.append(coarse_src[c, g, t] + cface * s)
                    out = sym([coarse_inv[i, g, t] for i in range(6)], flows)
                    result.append(
                        [(1.0 - damping) * now[g * GT + t][c] + out[c] for c in range(3)]
                    )
            return result

        current = lax.fori_loop(0, COARSE_SWEEPS - 1, coarse_turn, current)
        ratio = NM
        step = (lane // 2) & 3
        lane_far = jnp.where((step == 0) | (step == 3), 0.375, 0.125)
        sub_far = jnp.where(((sub // 2) == 0) | ((sub // 2) == 3), 0.375, 0.125)
        for g in range(GX):
            for t in range(GT):
                for c in range(3):
                    v = current[g * GT + t][c]
                    other = jnp.where(step < 2, zdn(v, 8), zup(v, 8))
                    corr[c, 2 + g, 8 + 8 * t:16 + 8 * t, :] = (1.0 - lane_far) * v + lane_far * other
        for c in range(3):
            columns = []
            for i in range(5):
                cells = [
                    jnp.broadcast_to(corr[c, gx + i, pl.ds(gy + 6 + j, 1), :], shape)
                    for j in range(5)
                ]
                columns.append([
                    (1.0 - sub_far) * cells[j] + sub_far * jnp.where(sub < 4, cells[j - 1], cells[j + 1])
                    for j in (1, 2, 3)
                ])
            for r in range(WR):
                b, d = r // ratio + 1, r % ratio
                shift = (d + 0.5) / ratio - 0.5
                o = b - 1 if shift < 0 else b + 1
                for j in range(3):
                    lifted = (1.0 - abs(shift)) * columns[b][j] + abs(shift) * columns[o][j]
                    err[p, c, r, j] = err[p, c, r, j] + lifted
        for sweep in range(1, SWEEPS + 1):
            mid_relax(p, sweep)
            p = 1 - p
        block_start(
            [[err[p, c, NM + r, 1] for r in range(NM)] for c in range(3)], bbase + 3
        )
        block_wait(3, bbase + 3)
        block_spread([err.at[p, c] for c in range(3)], bbase + 3)
        for c in range(3):
            raised = []
            for r in range(NM - 1, 2 * NM + 1):
                tiles = [err[p, c, r, j] for j in range(3)]
                ups, downs = y_shifts(tiles, 2)
                v = 0.75 * tiles[1] + 0.25 * jnp.where(sub_bit(1), downs[1], ups[1])
                v = 0.75 * v + 0.25 * jnp.where(lane_bit(1), zdn(v, 2), zup(v, 2))
                raised.append(v)
            for x in range(NR):
                m = x // 2 + 1
                o = m - 1 if x % 2 == 0 else m + 1
                flow_ref[c, x] = flow_ref[c, x] + 0.75 * raised[m] + 0.25 * raised[o]
        for sweep in range(SWEEPS):
            slot = base + 2 + SWEEPS + sweep
            fine_start(flow_ref, 3, slot)
            fine_wait(flow_ref, 3, slot)
            fine_relax(slot)
        return carry

    lax.fori_loop(0, CYCLES, cycle, 0)


def solution(mesh):
    GX, GY = mesh.shape["gx"], mesh.shape["gy"]

    def body(first_image, second_image, start_flow):
        NR, cols, depth = first_image.shape
        assert NR == 8 and cols == 8 and depth == 128 and GY % 8 == 0
        rounds = 1 + CYCLES * FINE_ROUNDS
        blocks = 1 + CYCLES * BLOCK_ROUNDS
        WR = 3 * NR // 2
        f32 = jnp.float32
        tile = (8, 128)
        vmem = lambda *front: pltpu.VMEM(front + tile, f32)
        return pl.pallas_call(
            functools.partial(kernel, GX, GY, NR),
            out_shape=jax.ShapeDtypeStruct(start_flow.shape, f32),
            in_specs=[pl.BlockSpec(memory_space=pltpu.VMEM)] * 3,
            out_specs=pl.BlockSpec(memory_space=pltpu.VMEM),
            scratch_shapes=[
                vmem(1, NR), vmem(1, NR), vmem(6, NR), vmem(3, NR), vmem(6, NR), vmem(6, NR),
                vmem(6, WR, 3), vmem(WR, 3), vmem(6, WR, 3), vmem(6, WR, 3), vmem(3, WR, 3),
                vmem(2, 3, WR, 3),
                vmem(6, GX, GY // 8), vmem(3, GX, GY // 8),
                pltpu.VMEM((3, GX + 4, GY + 16, 128), f32),
                vmem(rounds, 2, 3), vmem(rounds, 2, 3), vmem(rounds, 2, 3),
                vmem(blocks, 6), vmem(blocks, 8, 6),
                pltpu.VMEM((1 + CYCLES, 1, 128), f32),
                pltpu.VMEM((1 + CYCLES, GX * GY, 1, 128), f32),
                pltpu.SemaphoreType.DMA((rounds, 4)), pltpu.SemaphoreType.DMA((rounds, 4)),
                pltpu.SemaphoreType.DMA((blocks, 8)), pltpu.SemaphoreType.DMA((blocks, 8)),
                pltpu.SemaphoreType.DMA((1 + CYCLES,)), pltpu.SemaphoreType.DMA((1 + CYCLES,)),
            ],
            compiler_params=pltpu.CompilerParams(
                collective_id=0, has_side_effects=True, vmem_limit_bytes=48 * 1024 * 1024
            ),
            name="flow_cycles",
        )(first_image, second_image, start_flow)

    return jax.shard_map(
        body,
        mesh=mesh,
        in_specs=(P("gx", "gy", None), P("gx", "gy", None), P(None, "gx", "gy", None)),
        out_specs=P(None, "gx", "gy", None),
        check_vma=False,
    )
```

```python
import functools

import jax
import jax.numpy as jnp
from jax import lax
from jax.experimental import pallas as pl
from jax.experimental.pallas import tpu as pltpu
from jax.sharding import PartitionSpec as P

SWEEPS = 4
COARSE_SWEEPS = 12
CYCLES = 2
damping = 0.6
smooth_weight = 2.0
edge_scale = 0.25
floor_grad = 0.5
TINY = 1e-30

MESH = pl.DeviceIdType.MESH
SIDES = ((-1, 0), (1, 0), (0, -1), (0, 1))
AROUND = tuple((i, j) for i in (-1, 0, 1) for j in (-1, 0, 1) if (i, j) != (0, 0))
FINE_ROUNDS = 2 + 2 * SWEEPS
BLOCK_ROUNDS = 4


def sym(m, v):
    return [
        m[0] * v[0] + m[1] * v[1] + m[2] * v[2],
        m[1] * v[0] + m[3] * v[1] + m[4] * v[2],
        m[2] * v[0] + m[4] * v[1] + m[5] * v[2],
    ]


def damped_inverse(t, total):
    a, b, c, d, e, f = t[0] + total, t[1], t[2], t[3] + total, t[4], t[5] + total
    cof = [
        d * f - e * e,
        c * e - b * f,
        b * e - c * d,
        a * f - c * c,
        b * c - a * e,
        a * d - b * b,
    ]
    det = a * cof[0] + b * cof[1] + c * cof[2]
    factor = damping / jnp.where(total > 0.0, det, 1.0)
    return [factor * value for value in cof]


def kernel(
    GX, GY, NR, first_ref, second_ref, start_ref, flow_ref,
    mean_ref, weight_ref, tensor_ref, source_ref, face_ref, inv_ref,
    mid_t, mid_w, mid_face, mid_inv, mid_src, err,
    coarse_inv, coarse_src, corr,
    xh, yh, xs, ys, bs, br, gs, gb,
    f_send, f_recv, b_send, b_recv, g_send, g_recv,
):
    gx = lax.axis_index("gx")
    gy = lax.axis_index("gy")
    me = gx * GY + gy
    n = GX * GY
    GT = GY // 8
    NM = NR // 2
    WR = 3 * NM
    shape = (8, 128)
    lane = lax.broadcasted_iota(jnp.int32, shape, 1)
    sub = lax.broadcasted_iota(jnp.int32, shape, 0)
    zero = jnp.zeros(shape, jnp.float32)

    def lroll(v, k):
        return pltpu.roll(v, k % 128, 1)

    def sroll(v, k):
        return pltpu.roll(v, k % 8, 0)

    def lane_bit(k):
        return (lane & k) == 0

    def sub_bit(k):
        return (sub & k) == 0

    def lane_pair(v, k):
        return v + jnp.where(lane_bit(k), lroll(v, -k), lroll(v, k))

    def sub_pair(v, k):
        return v + jnp.where(sub_bit(k), sroll(v, -k), sroll(v, k))

    def zup(v, k):
        return jnp.where(lane < 128 - k, lroll(v, -k), 0.0)

    def zdn(v, k):
        return jnp.where(lane >= k, lroll(v, k), 0.0)

    def y_shifts(tiles, k):
        count = len(tiles)
        ups = [sroll(v, -k) for v in tiles] + [zero]
        downs = [zero] + [sroll(v, k) for v in tiles]
        return (
            [jnp.where(sub < 8 - k, ups[j], ups[j + 1]) for j in range(count)],
            [jnp.where(sub >= k, downs[j + 1], downs[j]) for j in range(count)],
        )

    def here(dx, dy):
        conds = []
        if dx:
            conds.append((gx + dx >= 0) & (gx + dx < GX))
        if dy:
            conds.append((gy + dy >= 0) & (gy + dy < GY))
        return functools.reduce(lambda p, q: p & q, conds)

    for ref in (xh, yh, br, corr):
        flat = 1
        for extent in ref.shape[:-2]:
            flat *= extent
        ref[...] = jnp.zeros(ref.shape, jnp.float32)

    barrier = pltpu.get_barrier_semaphore()

    def greet(d, carry):
        other = lax.rem(me + d, n)
        pl.semaphore_signal(
            barrier, inc=1, device_id=(other // GY, lax.rem(other, GY)), device_id_type=MESH
        )
        return carry

    lax.fori_loop(1, n, greet, 0)
    pl.semaphore_wait(barrier, n - 1)

    def side_copy(ref, count, slot, k):
        dx, dy = SIDES[k]
        back = k ^ 1
        if dx:
            src = xs.at[slot, k, pl.ds(0, count)]
            dst = xh.at[slot, back, pl.ds(0, count)]
        else:
            src = ys.at[slot, k - 2, pl.ds(0, count)]
            dst = yh.at[slot, back - 2, pl.ds(0, count)]
        return pltpu.make_async_remote_copy(
            src_ref=src, dst_ref=dst,
            send_sem=f_send.at[slot, k], recv_sem=f_recv.at[slot, back],
            device_id=(gx + dx, gy + dy), device_id_type=MESH,
        )

    def side_arrival(ref, count, slot, k):
        dx, dy = SIDES[k]
        if dx:
            dst = xh.at[slot, k, pl.ds(0, count)]
        else:
            dst = yh.at[slot, k - 2, pl.ds(0, count)]
        return pltpu.make_async_remote_copy(
            src_ref=dst, dst_ref=dst,
            send_sem=f_send.at[slot, k], recv_sem=f_recv.at[slot, k],
            device_id=(gx + dx, gy + dy), device_id_type=MESH,
        )

    def fine_start(ref, count, slot):
        for c in range(count):
            ys[slot, 0, c] = ref[c, :, 0, :]
            ys[slot, 1, c] = ref[c, :, 7, :]
            xs[slot, 0, c] = ref[c, 0]
            xs[slot, 1, c] = ref[c, NR - 1]
        for k in (2, 3, 0, 1):
            @pl.when(here(*SIDES[k]))
            def _(k=k):
                side_copy(ref, count, slot, k).start()

    def fine_wait(ref, count, slot):
        for k in (0, 1, 2, 3):
            @pl.when(here(*SIDES[k]))
            def _(k=k):
                side_arrival(ref, count, slot, k).wait_recv()
                side_copy(ref, count, slot, k).wait_send()

    def block_copy(count, slot, k):
        dx, dy = AROUND[k]
        return pltpu.make_async_remote_copy(
            src_ref=bs.at[slot, pl.ds(0, count)],
            dst_ref=br.at[slot, 7 - k, pl.ds(0, count)],
            send_sem=b_send.at[slot, k], recv_sem=b_recv.at[slot, 7 - k],
            device_id=(gx + dx, gy + dy), device_id_type=MESH,
        )

    def block_arrival(count, slot, k):
        dx, dy = AROUND[k]
        dst = br.at[slot, k, pl.ds(0, count)]
        return pltpu.make_async_remote_copy(
            src_ref=dst, dst_ref=dst,
            send_sem=b_send.at[slot, k], recv_sem=b_recv.at[slot, k],
            device_id=(gx + dx, gy + dy), device_id_type=MESH,
        )

    def pack(rows):
        lower = jnp.where(lane_bit(1), rows[0], rows[1])
        upper = jnp.where(lane_bit(1), rows[2], rows[3])
        return jnp.where(sub_bit(1), lower, upper)

    def unpack(v):
        even = jnp.where(lane_bit(1), v, lroll(v, 1))
        odd = jnp.where(lane_bit(1), lroll(v, -1), v)

        def split(w):
            return (
                jnp.where(sub_bit(1), w, sroll(w, 1)),
                jnp.where(sub_bit(1), sroll(w, -1), w),
            )

        e, o = split(even), split(odd)
        return [e[0], o[0], e[1], o[1]]

    def block_start(fields, slot):
        for i, rows in enumerate(fields):
            bs[slot, i] = pack(rows)
        for k in range(8):
            @pl.when(here(*AROUND[k]))
            def _(k=k):
                block_copy(len(fields), slot, k).start()

    def block_wait(count, slot):
        for k in range(8):
            @pl.when(here(*AROUND[k]))
            def _(k=k):
                block_arrival(count, slot, k).wait_recv()
                block_copy(count, slot, k).wait_send()

    def block_spread(places, slot):
        for k, (dx, dy) in enumerate(AROUND):
            for i, place in enumerate(places):
                for r, v in enumerate(unpack(br[slot, k, i])):
                    place[NM * (dx + 1) + r, dy + 1] = v

    def keep_own(place, rows):
        for r, v in enumerate(rows):
            place[NM + r, 1] = v

    def gather_copy(slot, other):
        return pltpu.make_async_remote_copy(
            src_ref=gs.at[slot], dst_ref=gb.at[slot, me],
            send_sem=g_send.at[slot], recv_sem=g_recv.at[slot],
            device_id=(other // GY, lax.rem(other, GY)), device_id_type=MESH,
        )

    def gather_start(values, slot):
        row = zero
        for i, v in enumerate(values):
            row = jnp.where((lane & 7) == i, v, row)
        gs[slot] = row[0:1]
        gb[slot, me] = row[0:1]

        def send(d, carry):
            gather_copy(slot, lax.rem(me + d, n)).start()
            return carry

        lax.fori_loop(1, n, send, 0)

    def gather_wait(slot):
        whole = gb.at[slot, pl.ds(0, n - 1)]
        copy = pltpu.make_async_remote_copy(
            src_ref=whole, dst_ref=whole,
            send_sem=g_send.at[slot], recv_sem=g_recv.at[slot],
            device_id=(gx, gy), device_id_type=MESH,
        )
        copy.wait_recv()
        copy.wait_send()

    def gathered(slot, count, g, t):
        packed = gb[slot, pl.ds(g * GY + t * 8, 8), 0, :]
        result = []
        for i in range(count):
            v = jnp.where((lane & 7) == i, packed, 0.0)
            for k in (1, 2, 4):
                v = lane_pair(v, k)
            result.append(v)
        return result

    def restrict_fine(rows):
        result = []
        for m in range(NM):
            v = rows[2 * m] + rows[2 * m + 1]
            result.append(sub_pair(lane_pair(v, 1), 1) * 0.125)
        return result

    def restrict_mid(rows):
        v = functools.reduce(lambda p, q: p + q, rows)
        for k in (2, 4):
            v = lane_pair(v, k)
            v = sub_pair(v, k)
        return v * (1.0 / 64.0)

    def fine_rows(ref, c, slot):
        return [xh[slot, 0, c]] + [ref[c, x] for x in range(NR)] + [xh[slot, 1, c]]

    def fine_y(rows, c, slot, x):
        v = rows[x + 1]
        up = jnp.where(sub < 7, sroll(v, -1), yh[slot, 1, c, x:x + 1, :])
        down = jnp.where(sub >= 1, sroll(v, 1), yh[slot, 0, c, x:x + 1, :])
        return up, down

    for x in range(NR):
        mean_ref[0, x] = 0.5 * (first_ref[x] + second_ref[x])
        for c in range(3):
            flow_ref[c, x] = start_ref[c, x]
    fine_start(mean_ref, 1, 0)
    fine_start(flow_ref, 3, 1)
    fine_wait(mean_ref, 1, 0)
    rows = fine_rows(mean_ref, 0, 0)
    for x in range(NR):
        up, down = fine_y(rows, 0, 0, x)
        s0 = 0.5 * (rows[x + 2] - rows[x])
        s1 = 0.5 * (up - down)
        s2 = 0.5 * (zup(rows[x + 1], 1) - zdn(rows[x + 1], 1))
        change = second_ref[x] - first_ref[x]
        scale = 1.0 / (s0 * s0 + s1 * s1 + s2 * s2 + floor_grad)
        a0, a1, a2 = scale * s0, scale * s1, scale * s2
        for i, v in enumerate((a0 * s0, a0 * s1, a0 * s2, a1 * s1, a1 * s2, a2 * s2)):
            tensor_ref[i, x] = v
        for i, v in enumerate((a0, a1, a2)):
            source_ref[i, x] = -v * change
    mids, coarses = [], []
    for i in range(6):
        own = restrict_fine([tensor_ref[i, x] for x in range(NR)])
        keep_own(mid_t.at[i], own)
        mids.append(own)
        coarses.append(restrict_mid(own))
    block_start(mids, 0)
    gather_start(coarses, 0)
    cface = smooth_weight / 64.0

    def mid_arrives():
        block_wait(6, 0)
        block_spread([mid_t.at[i] for i in range(6)], 0)

    def coarse_arrives():
        gather_wait(0)
        for g in range(GX):
            coarse_row(g)

    def coarse_row(g):
        for t in range(GT):
            tensor = gathered(0, 6, g, t)
            count = jnp.where(lane < 120, 1.0, 0.0) + jnp.where(lane >= 8, 1.0, 0.0)
            count = count + jnp.where(sub + t * 8 < GY - 1, 1.0, 0.0)
            count = count + jnp.where(sub + t * 8 >= 1, 1.0, 0.0)
            count = count + float((g > 0) + (g < GX - 1))
            for i, v in enumerate(damped_inverse(tensor, cface * count)):
                coarse_inv[i, g, t] = v

    def fine_inflow(x, all_rows, slot):
        flows = []
        face = [face_ref[i, x] for i in range(6)]
        for c in range(3):
            rows = all_rows[c]
            up, down = fine_y(rows, c, slot, x)
            v = source_ref[c, x] + face[0] * rows[x + 2] + face[1] * rows[x]
            v = v + face[2] * up + face[3] * down
            v = v + face[4] * lroll(rows[x + 1], -1) + face[5] * lroll(rows[x + 1], 1)
            flows.append(v)
        return flows, face

    def fine_inside():
        rows = [[flow_ref[c, x] for x in range(NR)] for c in range(3)]
        for x in range(NR):
            flows = []
            for c in range(3):
                now = rows[c][x]
                v = source_ref[c, x] + face_ref[4, x] * lroll(now, -1)
                v = v + face_ref[5, x] * lroll(now, 1)
                v = v + face_ref[2, x] * jnp.where(sub < 7, sroll(now, -1), 0.0)
                v = v + face_ref[3, x] * jnp.where(sub >= 1, sroll(now, 1), 0.0)
                if x < NR - 1:
                    v = v + face_ref[0, x] * rows[c][x + 1]
                if x > 0:
                    v = v + face_ref[1, x] * rows[c][x - 1]
                flows.append(v)
            out = sym([inv_ref[i, x] for i in range(6)], flows)
            for c in range(3):
                flow_ref[c, x] = (1.0 - damping) * rows[c][x] + out[c]

    def fine_edges(slot):
        for side, x, face in ((0, 0, 1), (1, NR - 1, 0)):
            outer = [face_ref[face, x] * xh[slot, side, c] for c in range(3)]
            out = sym([inv_ref[i, x] for i in range(6)], outer)
            for c in range(3):
                flow_ref[c, x] = flow_ref[c, x] + out[c]
        for side, y, face in ((0, 0, 3), (1, 7, 2)):
            outer = [face_ref[face, :, y, :] * yh[slot, side, c] for c in range(3)]
            out = sym([inv_ref[i, :, y, :] for i in range(6)], outer)
            for c in range(3):
                flow_ref[c, :, y, :] = flow_ref[c, :, y, :] + out[c]

    def mid_inflow(r, p, tiles, wanted):
        flows = [[None] * 3 for _ in range(3)]
        for c in range(3):
            now = [err[p, c, r, j] for j in range(3)]
            tiles[c] = now
            ups, downs = y_shifts(now, 2)
            for j in wanted:
                v = mid_src[c, r, j] + mid_face[0, r, j] * err[p, c, r + 1, j]
                v = v + mid_face[1, r, j] * err[p, c, r - 1, j]
                v = v + mid_face[2, r, j] * ups[j] + mid_face[3, r, j] * downs[j]
                v = v + mid_face[4, r, j] * lroll(now[j], -2)
                flows[c][j] = v + mid_face[5, r, j] * lroll(now[j], 2)
        return flows

    def mid_relax(p, low):
        def turn(r, carry):
            r = low + 2 * r
            done = []
            for u in range(2):
                tiles = [None] * 3
                flows = mid_inflow(r + u, p, tiles, (0, 1, 2))
                for j in range(3):
                    matrix = [mid_inv[i, r + u, j] for i in range(6)]
                    out = sym(matrix, [flows[c][j] for c in range(3)])
                    for c in range(3):
                        done.append((c, u, j, (1.0 - damping) * tiles[c][j] + out[c]))
            for c, u, j, v in done:
                err[1 - p, c, r + u, j] = v
            return carry

        lax.fori_loop(0, (WR - 2 * low) // 2, turn, 0)

    def mid_prepare():
        scale = 2.0 * smooth_weight / 4.0

        def turn(r, carry):
            now = [mid_w[r, j] for j in range(3)]
            has_up = jnp.where(r < WR - 1, 1.0, 0.0)
            has_down = jnp.where(r > 0, 1.0, 0.0)
            above = jnp.minimum(r + 1, WR - 1)
            below = jnp.maximum(r - 1, 0)
            ups, downs = y_shifts(now, 2)
            for j in range(3):
                v = now[j]
                beside = [
                    mid_w[above, j] * has_up, mid_w[below, j] * has_down,
                    ups[j], downs[j], zup(v, 2), zdn(v, 2),
                ]
                face = [scale * v * o / jnp.maximum(v + o, TINY) for o in beside]
                total = functools.reduce(lambda p, q: p + q, face)
                for i in range(6):
                    mid_face[i, r, j] = face[i]
                tensor = [mid_t[i, r, j] for i in range(6)]
                for i, w in enumerate(damped_inverse(tensor, total)):
                    mid_inv[i, r, j] = w
            return carry

        lax.fori_loop(0, WR, turn, 0)

    def cycle(cyc, carry):
        base = 1 + cyc * FINE_ROUNDS
        bbase = 1 + cyc * BLOCK_ROUNDS

        @pl.when(cyc > 0)
        def _():
            fine_start(flow_ref, 3, base)

        fine_wait(flow_ref, 3, base)
        q = [zero] * NR
        for c in range(3):
            rows = fine_rows(flow_ref, c, base)
            for x in range(NR):
                up, down = fine_y(rows, c, base, x)
                s0 = 0.5 * (rows[x + 2] - rows[x])
                s1 = 0.5 * (up - down)
                s2 = 0.5 * (zup(rows[x + 1], 1) - zdn(rows[x + 1], 1))
                q[x] = q[x] + s0 * s0 + s1 * s1 + s2 * s2
        weights = [lax.rsqrt(1.0 + v * (1.0 / edge_scale)) for v in q]
        for x in range(NR):
            weight_ref[0, x] = weights[x]
        fine_start(weight_ref, 1, base + 1)
        own_w = restrict_fine(weights)
        keep_own(mid_w, own_w)
        block_start([own_w], bbase)
        fine_wait(weight_ref, 1, base + 1)
        rows = fine_rows(weight_ref, 0, base + 1)
        for x in range(NR):
            v = rows[x + 1]
            up, down = fine_y(rows, 0, base + 1, x)
            beside = [rows[x + 2], rows[x], up, down, zup(v, 1), zdn(v, 1)]
            face = [2.0 * smooth_weight * v * o / (v + o) for o in beside]
            total = functools.reduce(lambda p, q: p + q, face)
            for i in range(6):
                face_ref[i, x] = face[i]
            tensor = [tensor_ref[i, x] for i in range(6)]
            for i, w in enumerate(damped_inverse(tensor, total)):
                inv_ref[i, x] = w
        fine_inside()
        fine_edges(base)
        for sweep in range(1, SWEEPS):
            slot = base + 1 + sweep
            fine_start(flow_ref, 3, slot)
            fine_inside()
            if sweep == 1:
                block_wait(1, bbase)
                block_spread([mid_w], bbase)
                pl.when(cyc == 0)(mid_arrives)
            if sweep == 2:
                mid_prepare()
            if sweep == 3:
                pl.when(cyc == 0)(coarse_arrives)
            fine_wait(flow_ref, 3, slot)
            fine_edges(slot)
        slot = base + 1 + SWEEPS
        fine_start(flow_ref, 3, slot)
        fine_wait(flow_ref, 3, slot)
        all_rows = [fine_rows(flow_ref, c, slot) for c in range(3)]
        rest = [[], [], []]
        for x in range(NR):
            flows, face = fine_inflow(x, all_rows, slot)
            total = functools.reduce(lambda p, q: p + q, face)
            now = [all_rows[c][x + 1] for c in range(3)]
            out = sym([tensor_ref[i, x] for i in range(6)], now)
            for c in range(3):
                rest[c].append(flows[c] - out[c] - total * now[c])
        srcs = [restrict_fine(rest[c]) for c in range(3)]
        errs = [[], [], []]
        for r in range(NM):
            out = sym([mid_inv[i, NM + r, 1] for i in range(6)], [srcs[c][r] for c in range(3)])
            for c in range(3):
                errs[c].append(out[c])
        block_start(srcs + errs, bbase + 1)
        for c in range(3):
            keep_own(mid_src.at[c], srcs[c])
            keep_own(err.at[0, c], errs[c])
        block_wait(6, bbase + 1)
        block_spread([mid_src.at[c] for c in range(3)] + [err.at[0, c] for c in range(3)], bbase + 1)
        p = 0
        for sweep in range(1, SWEEPS):
            mid_relax(p, sweep)
            p = 1 - p
        mrest = [[], [], []]
        olds = [[], [], []]
        for r in range(NM, 2 * NM):
            tiles = [None] * 3
            flows = mid_inflow(r, p, tiles, (1,))
            total = functools.reduce(lambda a, b: a + b, [mid_face[i, r, 1] for i in range(6)])
            now = [tiles[c][1] for c in range(3)]
            out = sym([mid_t[i, r, 1] for i in range(6)], now)
            for c in range(3):
                mrest[c].append(flows[c][1] - out[c] - total * now[c])
                olds[c].append(now[c])
        gather_start([restrict_mid(mrest[c]) for c in range(3)], 1 + cyc)
        block_start(olds, bbase + 2)
        block_wait(3, bbase + 2)
        block_spread([err.at[p, c] for c in range(3)], bbase + 2)
        gather_wait(1 + cyc)

        current = []
        for g in range(GX):
            for t in range(GT):
                src = gathered(1 + cyc, 3, g, t)
                out = sym([coarse_inv[i, g, t] for i in range(6)], src)
                for c in range(3):
                    coarse_src[c, g, t] = src[c]
                current.append(out)

        def coarse_turn(index, now):
            result = []
            for g in range(GX):
                shifted = [
                    y_shifts([now[g * GT + t][c] for t in range(GT)], 1) for c in range(3)
                ]
                for t in range(GT):
                    flows = []
                    for c in range(3):
                        v = now[g * GT + t][c]
                        s = shifted[c][0][t] + shifted[c][1][t]
                        s = s + (zup(v, 8) + zdn(v, 8))
                        if g > 0:
                            s = s + now[(g - 1) * GT + t][c]
                        if g < GX - 1:
                            s = s + now[(g + 1) * GT + t][c]
                        flows.append(coarse_src[c, g, t] + cface * s)
                    out = sym([coarse_inv[i, g, t] for i in range(6)], flows)
                    result.append(
                        [(1.0 - damping) * now[g * GT + t][c] + out[c] for c in range(3)]
                    )
            return result

        current = lax.fori_loop(0, COARSE_SWEEPS - 1, coarse_turn, current)
        ratio = NM
        step = (lane // 2) & 3
        lane_far = jnp.where((step == 0) | (step == 3), 0.375, 0.125)
        sub_far = jnp.where(((sub // 2) == 0) | ((sub // 2) == 3), 0.375, 0.125)
        for g in range(GX):
            for t in range(GT):
                for c in range(3):
                    v = current[g * GT + t][c]
                    other = jnp.where(step < 2, zdn(v, 8), zup(v, 8))
                    corr[c, 2 + g, 8 + 8 * t:16 + 8 * t, :] = (1.0 - lane_far) * v + lane_far * other
        for c in range(3):
            columns = []
            for i in range(5):
                cells = [
                    jnp.broadcast_to(corr[c, gx + i, pl.ds(gy + 6 + j, 1), :], shape)
                    for j in range(5)
                ]
                columns.append([
                    (1.0 - sub_far) * cells[j] + sub_far * jnp.where(sub < 4, cells[j - 1], cells[j + 1])
                    for j in (1, 2, 3)
                ])
            for r in range(WR):
                b, d = r // ratio + 1, r % ratio
                shift = (d + 0.5) / ratio - 0.5
                o = b - 1 if shift < 0 else b + 1
                for j in range(3):
                    lifted = (1.0 - abs(shift)) * columns[b][j] + abs(shift) * columns[o][j]
                    err[p, c, r, j] = err[p, c, r, j] + lifted
        for sweep in range(1, SWEEPS + 1):
            mid_relax(p, sweep)
            p = 1 - p
        block_start(
            [[err[p, c, NM + r, 1] for r in range(NM)] for c in range(3)], bbase + 3
        )
        block_wait(3, bbase + 3)
        block_spread([err.at[p, c] for c in range(3)], bbase + 3)
        for c in range(3):
            raised = []
            for r in range(NM - 1, 2 * NM + 1):
                tiles = [err[p, c, r, j] for j in range(3)]
                ups, downs = y_shifts(tiles, 2)
                v = 0.75 * tiles[1] + 0.25 * jnp.where(sub_bit(1), downs[1], ups[1])
                v = 0.75 * v + 0.25 * jnp.where(lane_bit(1), zdn(v, 2), zup(v, 2))
                raised.append(v)
            for x in range(NR):
                m = x // 2 + 1
                o = m - 1 if x % 2 == 0 else m + 1
                flow_ref[c, x] = flow_ref[c, x] + 0.75 * raised[m] + 0.25 * raised[o]
        for sweep in range(SWEEPS):
            slot = base + 2 + SWEEPS + sweep
            fine_start(flow_ref, 3, slot)
            fine_inside()
            fine_wait(flow_ref, 3, slot)
            fine_edges(slot)
        return carry

    lax.fori_loop(0, CYCLES, cycle, 0)


def solution(mesh):
    GX, GY = mesh.shape["gx"], mesh.shape["gy"]

    def body(first_image, second_image, start_flow):
        NR, cols, depth = first_image.shape
        assert NR == 8 and cols == 8 and depth == 128 and GY % 8 == 0
        rounds = 1 + CYCLES * FINE_ROUNDS
        blocks = 1 + CYCLES * BLOCK_ROUNDS
        WR = 3 * NR // 2
        f32 = jnp.float32
        tile = (8, 128)
        vmem = lambda *front: pltpu.VMEM(front + tile, f32)
        return pl.pallas_call(
            functools.partial(kernel, GX, GY, NR),
            out_shape=jax.ShapeDtypeStruct(start_flow.shape, f32),
            in_specs=[pl.BlockSpec(memory_space=pltpu.VMEM)] * 3,
            out_specs=pl.BlockSpec(memory_space=pltpu.VMEM),
            scratch_shapes=[
                vmem(1, NR), vmem(1, NR), vmem(6, NR), vmem(3, NR), vmem(6, NR), vmem(6, NR),
                vmem(6, WR, 3), vmem(WR, 3), vmem(6, WR, 3), vmem(6, WR, 3), vmem(3, WR, 3),
                vmem(2, 3, WR, 3),
                vmem(6, GX, GY // 8), vmem(3, GX, GY // 8),
                pltpu.VMEM((3, GX + 4, GY + 16, 128), f32),
                vmem(rounds, 2, 3), vmem(rounds, 2, 3), vmem(rounds, 2, 3), vmem(rounds, 2, 3),
                vmem(blocks, 6), vmem(blocks, 8, 6),
                pltpu.VMEM((1 + CYCLES, 1, 128), f32),
                pltpu.VMEM((1 + CYCLES, GX * GY, 1, 128), f32),
                pltpu.SemaphoreType.DMA((rounds, 4)), pltpu.SemaphoreType.DMA((rounds, 4)),
                pltpu.SemaphoreType.DMA((blocks, 8)), pltpu.SemaphoreType.DMA((blocks, 8)),
                pltpu.SemaphoreType.DMA((1 + CYCLES,)), pltpu.SemaphoreType.DMA((1 + CYCLES,)),
            ],
            compiler_params=pltpu.CompilerParams(
                collective_id=0, has_side_effects=True, vmem_limit_bytes=48 * 1024 * 1024
            ),
            name="flow_cycles",
        )(first_image, second_image, start_flow)

    return jax.shard_map(
        body,
        mesh=mesh,
        in_specs=(P("gx", "gy", None), P("gx", "gy", None), P(None, "gx", "gy", None)),
        out_specs=P(None, "gx", "gy", None),
        check_vma=False,
    )
```

```python
import functools

import jax
import jax.numpy as jnp
from jax import lax
from jax.experimental import pallas as pl
from jax.experimental.pallas import tpu as pltpu
from jax.sharding import PartitionSpec as P

SWEEPS = 4
COARSE_SWEEPS = 12
CYCLES = 2
damping = 0.6
smooth_weight = 2.0
edge_scale = 0.25
floor_grad = 0.5
TINY = 1e-30

MESH = pl.DeviceIdType.MESH
SIDES = ((-1, 0), (1, 0), (0, -1), (0, 1))
AROUND = tuple((i, j) for i in (-1, 0, 1) for j in (-1, 0, 1) if (i, j) != (0, 0))
FINE_ROUNDS = 2 + 2 * SWEEPS
BLOCK_ROUNDS = 5


def sym(m, v):
    return [
        m[0] * v[0] + m[1] * v[1] + m[2] * v[2],
        m[1] * v[0] + m[3] * v[1] + m[4] * v[2],
        m[2] * v[0] + m[4] * v[1] + m[5] * v[2],
    ]


def damped_inverse(t, total):
    a, b, c, d, e, f = t[0] + total, t[1], t[2], t[3] + total, t[4], t[5] + total
    cof = [
        d * f - e * e,
        c * e - b * f,
        b * e - c * d,
        a * f - c * c,
        b * c - a * e,
        a * d - b * b,
    ]
    det = a * cof[0] + b * cof[1] + c * cof[2]
    factor = damping / jnp.where(total > 0.0, det, 1.0)
    return [factor * value for value in cof]


def kernel(
    GX, GY, NR, first_ref, second_ref, start_ref, flow_ref,
    mean_ref, weight_ref, tensor_ref, source_ref, face_ref, inv_ref,
    mid_t, mid_w, mid_total, mid_face, mid_inv, mid_src, err,
    coarse_inv, coarse_src, corr,
    xh, yh, xs, ys, bs, br, gs, gb,
    f_send, f_recv, b_send, b_recv, g_send, g_recv,
):
    gx = lax.axis_index("gx")
    gy = lax.axis_index("gy")
    me = gx * GY + gy
    n = GX * GY
    GT = GY // 8
    NM = NR // 2
    WR = 3 * NM
    shape = (8, 128)
    lane = lax.broadcasted_iota(jnp.int32, shape, 1)
    sub = lax.broadcasted_iota(jnp.int32, shape, 0)
    zero = jnp.zeros(shape, jnp.float32)

    def lroll(v, k):
        return pltpu.roll(v, k % 128, 1)

    def sroll(v, k):
        return pltpu.roll(v, k % 8, 0)

    def lane_bit(k):
        return (lane & k) == 0

    def sub_bit(k):
        return (sub & k) == 0

    def lane_pair(v, k):
        return v + jnp.where(lane_bit(k), lroll(v, -k), lroll(v, k))

    def sub_pair(v, k):
        return v + jnp.where(sub_bit(k), sroll(v, -k), sroll(v, k))

    def zup(v, k):
        return jnp.where(lane < 128 - k, lroll(v, -k), 0.0)

    def zdn(v, k):
        return jnp.where(lane >= k, lroll(v, k), 0.0)

    def y_shifts(tiles, k):
        count = len(tiles)
        ups = [sroll(v, -k) for v in tiles] + [zero]
        downs = [zero] + [sroll(v, k) for v in tiles]
        return (
            [jnp.where(sub < 8 - k, ups[j], ups[j + 1]) for j in range(count)],
            [jnp.where(sub >= k, downs[j + 1], downs[j]) for j in range(count)],
        )

    def here(dx, dy):
        conds = []
        if dx:
            conds.append((gx + dx >= 0) & (gx + dx < GX))
        if dy:
            conds.append((gy + dy >= 0) & (gy + dy < GY))
        return functools.reduce(lambda p, q: p & q, conds)

    for ref in (xh, yh, br, corr):
        flat = 1
        for extent in ref.shape[:-2]:
            flat *= extent
        ref[...] = jnp.zeros(ref.shape, jnp.float32)

    barrier = pltpu.get_barrier_semaphore()

    def greet(d, carry):
        other = lax.rem(me + d, n)
        pl.semaphore_signal(
            barrier, inc=1, device_id=(other // GY, lax.rem(other, GY)), device_id_type=MESH
        )
        return carry

    lax.fori_loop(1, n, greet, 0)
    pl.semaphore_wait(barrier, n - 1)

    def side_copy(ref, count, slot, k):
        dx, dy = SIDES[k]
        back = k ^ 1
        if dx:
            src = xs.at[slot, k, pl.ds(0, count)]
            dst = xh.at[slot, back, pl.ds(0, count)]
        else:
            src = ys.at[slot, k - 2, pl.ds(0, count)]
            dst = yh.at[slot, back - 2, pl.ds(0, count)]
        return pltpu.make_async_remote_copy(
            src_ref=src, dst_ref=dst,
            send_sem=f_send.at[slot, k], recv_sem=f_recv.at[slot, back],
            device_id=(gx + dx, gy + dy), device_id_type=MESH,
        )

    def side_arrival(ref, count, slot, k):
        dx, dy = SIDES[k]
        if dx:
            dst = xh.at[slot, k, pl.ds(0, count)]
        else:
            dst = yh.at[slot, k - 2, pl.ds(0, count)]
        return pltpu.make_async_remote_copy(
            src_ref=dst, dst_ref=dst,
            send_sem=f_send.at[slot, k], recv_sem=f_recv.at[slot, k],
            device_id=(gx + dx, gy + dy), device_id_type=MESH,
        )

    def fine_start(ref, count, slot):
        for c in range(count):
            ys[slot, 0, c] = ref[c, :, 0, :]
            ys[slot, 1, c] = ref[c, :, 7, :]
            xs[slot, 0, c] = ref[c, 0]
            xs[slot, 1, c] = ref[c, NR - 1]
        for k in (2, 3, 0, 1):
            @pl.when(here(*SIDES[k]))
            def _(k=k):
                side_copy(ref, count, slot, k).start()

    def fine_wait(ref, count, slot):
        for k in (0, 1, 2, 3):
            @pl.when(here(*SIDES[k]))
            def _(k=k):
                side_arrival(ref, count, slot, k).wait_recv()
                side_copy(ref, count, slot, k).wait_send()

    def block_copy(count, slot, k):
        dx, dy = AROUND[k]
        return pltpu.make_async_remote_copy(
            src_ref=bs.at[slot, pl.ds(0, count)],
            dst_ref=br.at[slot, 7 - k, pl.ds(0, count)],
            send_sem=b_send.at[slot, k], recv_sem=b_recv.at[slot, 7 - k],
            device_id=(gx + dx, gy + dy), device_id_type=MESH,
        )

    def block_arrival(count, slot, k):
        dx, dy = AROUND[k]
        dst = br.at[slot, k, pl.ds(0, count)]
        return pltpu.make_async_remote_copy(
            src_ref=dst, dst_ref=dst,
            send_sem=b_send.at[slot, k], recv_sem=b_recv.at[slot, k],
            device_id=(gx + dx, gy + dy), device_id_type=MESH,
        )

    def pack(rows):
        lower = jnp.where(lane_bit(1), rows[0], rows[1])
        upper = jnp.where(lane_bit(1), rows[2], rows[3])
        return jnp.where(sub_bit(1), lower, upper)

    def unpack(v):
        even = jnp.where(lane_bit(1), v, lroll(v, 1))
        odd = jnp.where(lane_bit(1), lroll(v, -1), v)

        def split(w):
            return (
                jnp.where(sub_bit(1), w, sroll(w, 1)),
                jnp.where(sub_bit(1), sroll(w, -1), w),
            )

        e, o = split(even), split(odd)
        return [e[0], o[0], e[1], o[1]]

    def block_start(fields, slot):
        for i, rows in enumerate(fields):
            bs[slot, i] = pack(rows)
        for k in range(8):
            @pl.when(here(*AROUND[k]))
            def _(k=k):
                block_copy(len(fields), slot, k).start()

    def block_wait(count, slot):
        for k in range(8):
            @pl.when(here(*AROUND[k]))
            def _(k=k):
                block_arrival(count, slot, k).wait_recv()
                block_copy(count, slot, k).wait_send()

    def block_spread(places, slot):
        for k, (dx, dy) in enumerate(AROUND):
            for i, place in enumerate(places):
                for r, v in enumerate(unpack(br[slot, k, i])):
                    place[NM * (dx + 1) + r, dy + 1] = v

    def keep_own(place, rows):
        for r, v in enumerate(rows):
            place[NM + r, 1] = v

    def gather_copy(slot, other):
        return pltpu.make_async_remote_copy(
            src_ref=gs.at[slot], dst_ref=gb.at[slot, me],
            send_sem=g_send.at[slot], recv_sem=g_recv.at[slot],
            device_id=(other // GY, lax.rem(other, GY)), device_id_type=MESH,
        )

    def gather_start(values, slot):
        row = zero
        for i, v in enumerate(values):
            row = jnp.where((lane & 7) == i, v, row)
        gs[slot] = row[0:1]
        gb[slot, me] = row[0:1]

        def send(d, carry):
            gather_copy(slot, lax.rem(me + d, n)).start()
            return carry

        lax.fori_loop(1, n, send, 0)

    def gather_wait(slot):
        whole = gb.at[slot, pl.ds(0, n - 1)]
        copy = pltpu.make_async_remote_copy(
            src_ref=whole, dst_ref=whole,
            send_sem=g_send.at[slot], recv_sem=g_recv.at[slot],
            device_id=(gx, gy), device_id_type=MESH,
        )
        copy.wait_recv()
        copy.wait_send()

    def gathered(slot, count, g, t):
        packed = gb[slot, pl.ds(g * GY + t * 8, 8), 0, :]
        result = []
        for i in range(count):
            v = jnp.where((lane & 7) == i, packed, 0.0)
            for k in (1, 2, 4):
                v = lane_pair(v, k)
            result.append(v)
        return result

    def restrict_fine(rows):
        result = []
        for m in range(NM):
            v = rows[2 * m] + rows[2 * m + 1]
            result.append(sub_pair(lane_pair(v, 1), 1) * 0.125)
        return result

    def restrict_mid(rows):
        v = functools.reduce(lambda p, q: p + q, rows)
        for k in (2, 4):
            v = lane_pair(v, k)
            v = sub_pair(v, k)
        return v * (1.0 / 64.0)

    def fine_rows(ref, c, slot):
        return [xh[slot, 0, c]] + [ref[c, x] for x in range(NR)] + [xh[slot, 1, c]]

    def fine_y(rows, c, slot, x):
        v = rows[x + 1]
        up = jnp.where(sub < 7, sroll(v, -1), yh[slot, 1, c, x:x + 1, :])
        down = jnp.where(sub >= 1, sroll(v, 1), yh[slot, 0, c, x:x + 1, :])
        return up, down

    for x in range(NR):
        mean_ref[0, x] = 0.5 * (first_ref[x] + second_ref[x])
        for c in range(3):
            flow_ref[c, x] = start_ref[c, x]
    fine_start(mean_ref, 1, 0)
    fine_start(flow_ref, 3, 1)
    fine_wait(mean_ref, 1, 0)
    rows = fine_rows(mean_ref, 0, 0)
    for x in range(NR):
        up, down = fine_y(rows, 0, 0, x)
        s0 = 0.5 * (rows[x + 2] - rows[x])
        s1 = 0.5 * (up - down)
        s2 = 0.5 * (zup(rows[x + 1], 1) - zdn(rows[x + 1], 1))
        change = second_ref[x] - first_ref[x]
        scale = 1.0 / (s0 * s0 + s1 * s1 + s2 * s2 + floor_grad)
        a0, a1, a2 = scale * s0, scale * s1, scale * s2
        for i, v in enumerate((a0 * s0, a0 * s1, a0 * s2, a1 * s1, a1 * s2, a2 * s2)):
            tensor_ref[i, x] = v
        for i, v in enumerate((a0, a1, a2)):
            source_ref[i, x] = -v * change
    mids, coarses = [], []
    for i in range(6):
        own = restrict_fine([tensor_ref[i, x] for x in range(NR)])
        keep_own(mid_t.at[i], own)
        mids.append(own)
        coarses.append(restrict_mid(own))
    block_start(mids, 0)
    gather_start(coarses, 0)
    cface = smooth_weight / 64.0

    def mid_arrives():
        block_wait(6, 0)
        block_spread([mid_t.at[i] for i in range(6)], 0)

    def coarse_arrives():
        gather_wait(0)
        for g in range(GX):
            coarse_row(g)

    def coarse_row(g):
        for t in range(GT):
            tensor = gathered(0, 6, g, t)
            count = jnp.where(lane < 120, 1.0, 0.0) + jnp.where(lane >= 8, 1.0, 0.0)
            count = count + jnp.where(sub + t * 8 < GY - 1, 1.0, 0.0)
            count = count + jnp.where(sub + t * 8 >= 1, 1.0, 0.0)
            count = count + float((g > 0) + (g < GX - 1))
            for i, v in enumerate(damped_inverse(tensor, cface * count)):
                coarse_inv[i, g, t] = v

    def fine_inflow(x, all_rows, slot):
        flows = []
        face = [face_ref[i, x] for i in range(6)]
        for c in range(3):
            rows = all_rows[c]
            up, down = fine_y(rows, c, slot, x)
            v = source_ref[c, x] + face[0] * rows[x + 2] + face[1] * rows[x]
            v = v + face[2] * up + face[3] * down
            v = v + face[4] * lroll(rows[x + 1], -1) + face[5] * lroll(rows[x + 1], 1)
            flows.append(v)
        return flows, face

    def fine_inside():
        rows = [[flow_ref[c, x] for x in range(NR)] for c in range(3)]
        for x in range(NR):
            flows = []
            for c in range(3):
                now = rows[c][x]
                v = source_ref[c, x] + face_ref[4, x] * lroll(now, -1)
                v = v + face_ref[5, x] * lroll(now, 1)
                v = v + face_ref[2, x] * jnp.where(sub < 7, sroll(now, -1), 0.0)
                v = v + face_ref[3, x] * jnp.where(sub >= 1, sroll(now, 1), 0.0)
                if x < NR - 1:
                    v = v + face_ref[0, x] * rows[c][x + 1]
                if x > 0:
                    v = v + face_ref[1, x] * rows[c][x - 1]
                flows.append(v)
            out = sym([inv_ref[i, x] for i in range(6)], flows)
            for c in range(3):
                flow_ref[c, x] = (1.0 - damping) * rows[c][x] + out[c]

    def fine_edges(slot):
        for side, x, face in ((0, 0, 1), (1, NR - 1, 0)):
            outer = [face_ref[face, x] * xh[slot, side, c] for c in range(3)]
            out = sym([inv_ref[i, x] for i in range(6)], outer)
            for c in range(3):
                flow_ref[c, x] = flow_ref[c, x] + out[c]
        for side, y, face in ((0, 0, 3), (1, 7, 2)):
            outer = [face_ref[face, :, y, :] * yh[slot, side, c] for c in range(3)]
            out = sym([inv_ref[i, :, y, :] for i in range(6)], outer)
            for c in range(3):
                flow_ref[c, :, y, :] = flow_ref[c, :, y, :] + out[c]

    def mid_inflow(r, p, tiles, wanted):
        flows = [[None] * 3 for _ in range(3)]
        for c in range(3):
            now = [err[p, c, r, j] for j in range(3)]
            tiles[c] = now
            ups, downs = y_shifts(now, 2)
            for j in wanted:
                v = mid_src[c, r, j] + mid_face[0, r, j] * err[p, c, r + 1, j]
                v = v + mid_face[1, r, j] * err[p, c, r - 1, j]
                v = v + mid_face[2, r, j] * ups[j] + mid_face[3, r, j] * downs[j]
                v = v + mid_face[4, r, j] * lroll(now[j], -2)
                flows[c][j] = v + mid_face[5, r, j] * lroll(now[j], 2)
        return flows

    def mid_relax(p, low):
        def turn(r, carry):
            r = low + 2 * r
            done = []
            for u in range(2):
                tiles = [None] * 3
                flows = mid_inflow(r + u, p, tiles, (0, 1, 2))
                for j in range(3):
                    matrix = [mid_inv[i, r + u, j] for i in range(6)]
                    out = sym(matrix, [flows[c][j] for c in range(3)])
                    for c in range(3):
                        done.append((c, u, j, (1.0 - damping) * tiles[c][j] + out[c]))
            for c, u, j, v in done:
                err[1 - p, c, r + u, j] = v
            return carry

        lax.fori_loop(0, (WR - 2 * low) // 2, turn, 0)

    def mid_prepare():
        scale = 2.0 * smooth_weight / 4.0

        def turn(r, carry):
            now = [mid_w[r, j] for j in range(3)]
            has_up = jnp.where(r < WR - 1, 1.0, 0.0)
            has_down = jnp.where(r > 0, 1.0, 0.0)
            above = jnp.minimum(r + 1, WR - 1)
            below = jnp.maximum(r - 1, 0)
            ups, downs = y_shifts(now, 2)
            for j in range(3):
                v = now[j]
                beside = [
                    mid_w[above, j] * has_up, mid_w[below, j] * has_down,
                    ups[j], downs[j], zup(v, 2), zdn(v, 2),
                ]
                face = [scale * v * o / jnp.maximum(v + o, TINY) for o in beside]
                total = functools.reduce(lambda p, q: p + q, face)
                for i in range(6):
                    mid_face[i, r, j] = face[i]
                mid_total[r, j] = total
            return carry

        lax.fori_loop(0, WR, turn, 0)

    def mid_invert():
        def turn(r, carry):
            for j in range(3):
                tensor = [mid_t[i, r, j] for i in range(6)]
                for i, w in enumerate(damped_inverse(tensor, mid_total[r, j])):
                    mid_inv[i, r, j] = w
            return carry

        lax.fori_loop(0, WR, turn, 0)

    def mid_begin():
        def turn(r, carry):
            for j in range(3):
                matrix = [mid_inv[i, r, j] for i in range(6)]
                out = sym(matrix, [mid_src[c, r, j] for c in range(3)])
                for c in range(3):
                    err[0, c, r, j] = out[c]
            return carry

        lax.fori_loop(0, WR, turn, 0)

    def cycle(cyc, carry):
        base = 1 + cyc * FINE_ROUNDS
        bbase = 1 + cyc * BLOCK_ROUNDS

        @pl.when(cyc > 0)
        def _():
            fine_start(flow_ref, 3, base)

        fine_wait(flow_ref, 3, base)
        q = [zero] * NR
        for c in range(3):
            rows = fine_rows(flow_ref, c, base)
            for x in range(NR):
                up, down = fine_y(rows, c, base, x)
                s0 = 0.5 * (rows[x + 2] - rows[x])
                s1 = 0.5 * (up - down)
                s2 = 0.5 * (zup(rows[x + 1], 1) - zdn(rows[x + 1], 1))
                q[x] = q[x] + s0 * s0 + s1 * s1 + s2 * s2
        weights = [lax.rsqrt(1.0 + v * (1.0 / edge_scale)) for v in q]
        for x in range(NR):
            weight_ref[0, x] = weights[x]
        fine_start(weight_ref, 1, base + 1)
        own_w = restrict_fine(weights)
        keep_own(mid_w, own_w)
        block_start([own_w], bbase)
        fine_wait(weight_ref, 1, base + 1)
        rows = fine_rows(weight_ref, 0, base + 1)
        for x in range(NR):
            v = rows[x + 1]
            up, down = fine_y(rows, 0, base + 1, x)
            beside = [rows[x + 2], rows[x], up, down, zup(v, 1), zdn(v, 1)]
            face = [2.0 * smooth_weight * v * o / (v + o) for o in beside]
            total = functools.reduce(lambda p, q: p + q, face)
            for i in range(6):
                face_ref[i, x] = face[i]
            tensor = [tensor_ref[i, x] for i in range(6)]
            for i, w in enumerate(damped_inverse(tensor, total)):
                inv_ref[i, x] = w
        fine_inside()
        fine_edges(base)
        for sweep in range(1, SWEEPS):
            slot = base + 1 + sweep
            fine_start(flow_ref, 3, slot)
            fine_inside()
            if sweep == 1:
                block_wait(1, bbase)
                block_spread([mid_w], bbase)
                pl.when(cyc == 0)(mid_arrives)
            if sweep == 2:
                mid_prepare()
                block_start([[mid_total[NM + r, 1] for r in range(NM)]], bbase + 4)
            if sweep == 3:
                block_wait(1, bbase + 4)
                block_spread([mid_total], bbase + 4)
                mid_invert()
                pl.when(cyc == 0)(coarse_arrives)
            fine_wait(flow_ref, 3, slot)
            fine_edges(slot)
        slot = base + 1 + SWEEPS
        fine_start(flow_ref, 3, slot)
        fine_wait(flow_ref, 3, slot)
        all_rows = [fine_rows(flow_ref, c, slot) for c in range(3)]
        rest = [[], [], []]
        for x in range(NR):
            flows, face = fine_inflow(x, all_rows, slot)
            total = functools.reduce(lambda p, q: p + q, face)
            now = [all_rows[c][x + 1] for c in range(3)]
            out = sym([tensor_ref[i, x] for i in range(6)], now)
            for c in range(3):
                rest[c].append(flows[c] - out[c] - total * now[c])
        srcs = [restrict_fine(rest[c]) for c in range(3)]
        block_start(srcs, bbase + 1)
        for c in range(3):
            keep_own(mid_src.at[c], srcs[c])
        block_wait(3, bbase + 1)
        block_spread([mid_src.at[c] for c in range(3)], bbase + 1)
        mid_begin()
        p = 0
        for sweep in range(1, SWEEPS):
            mid_relax(p, sweep)
            p = 1 - p
        mrest = [[], [], []]
        olds = [[], [], []]
        for r in range(NM, 2 * NM):
            tiles = [None] * 3
            flows = mid_inflow(r, p, tiles, (1,))
            total = functools.reduce(lambda a, b: a + b, [mid_face[i, r, 1] for i in range(6)])
            now = [tiles[c][1] for c in range(3)]
            out = sym([mid_t[i, r, 1] for i in range(6)], now)
            for c in range(3):
                mrest[c].append(flows[c][1] - out[c] - total * now[c])
                olds[c].append(now[c])
        gather_start([restrict_mid(mrest[c]) for c in range(3)], 1 + cyc)
        block_start(olds, bbase + 2)
        block_wait(3, bbase + 2)
        block_spread([err.at[p, c] for c in range(3)], bbase + 2)
        gather_wait(1 + cyc)

        current = []
        for g in range(GX):
            for t in range(GT):
                src = gathered(1 + cyc, 3, g, t)
                out = sym([coarse_inv[i, g, t] for i in range(6)], src)
                for c in range(3):
                    coarse_src[c, g, t] = src[c]
                current.append(out)

        def coarse_turn(index, now):
            result = []
            for g in range(GX):
                shifted = [
                    y_shifts([now[g * GT + t][c] for t in range(GT)], 1) for c in range(3)
                ]
                for t in range(GT):
                    flows = []
                    for c in range(3):
                        v = now[g * GT + t][c]
                        s = shifted[c][0][t] + shifted[c][1][t]
                        s = s + (zup(v, 8) + zdn(v, 8))
                        if g > 0:
                            s = s + now[(g - 1) * GT + t][c]
                        if g < GX - 1:
                            s = s + now[(g + 1) * GT + t][c]
                        flows.append(coarse_src[c, g, t] + cface * s)
                    out = sym([coarse_inv[i, g, t] for i in range(6)], flows)
                    result.append(
                        [(1.0 - damping) * now[g * GT + t][c] + out[c] for c in range(3)]
                    )
            return result

        current = lax.fori_loop(0, COARSE_SWEEPS - 1, coarse_turn, current)
        ratio = NM
        step = (lane // 2) & 3
        lane_far = jnp.where((step == 0) | (step == 3), 0.375, 0.125)
        sub_far = jnp.where(((sub // 2) == 0) | ((sub // 2) == 3), 0.375, 0.125)
        for g in range(GX):
            for t in range(GT):
                for c in range(3):
                    v = current[g * GT + t][c]
                    other = jnp.where(step < 2, zdn(v, 8), zup(v, 8))
                    corr[c, 2 + g, 8 + 8 * t:16 + 8 * t, :] = (1.0 - lane_far) * v + lane_far * other
        for c in range(3):
            columns = []
            for i in range(5):
                cells = [
                    jnp.broadcast_to(corr[c, gx + i, pl.ds(gy + 6 + j, 1), :], shape)
                    for j in range(5)
                ]
                columns.append([
                    (1.0 - sub_far) * cells[j] + sub_far * jnp.where(sub < 4, cells[j - 1], cells[j + 1])
                    for j in (1, 2, 3)
                ])
            for r in range(WR):
                b, d = r // ratio + 1, r % ratio
                shift = (d + 0.5) / ratio - 0.5
                o = b - 1 if shift < 0 else b + 1
                for j in range(3):
                    lifted = (1.0 - abs(shift)) * columns[b][j] + abs(shift) * columns[o][j]
                    err[p, c, r, j] = err[p, c, r, j] + lifted
        for sweep in range(1, SWEEPS + 1):
            mid_relax(p, sweep)
            p = 1 - p
        block_start(
            [[err[p, c, NM + r, 1] for r in range(NM)] for c in range(3)], bbase + 3
        )
        block_wait(3, bbase + 3)
        block_spread([err.at[p, c] for c in range(3)], bbase + 3)
        for c in range(3):
            raised = []
            for r in range(NM - 1, 2 * NM + 1):
                tiles = [err[p, c, r, j] for j in range(3)]
                ups, downs = y_shifts(tiles, 2)
                v = 0.75 * tiles[1] + 0.25 * jnp.where(sub_bit(1), downs[1], ups[1])
                v = 0.75 * v + 0.25 * jnp.where(lane_bit(1), zdn(v, 2), zup(v, 2))
                raised.append(v)
            for x in range(NR):
                m = x // 2 + 1
                o = m - 1 if x % 2 == 0 else m + 1
                flow_ref[c, x] = flow_ref[c, x] + 0.75 * raised[m] + 0.25 * raised[o]
        for sweep in range(SWEEPS):
            slot = base + 2 + SWEEPS + sweep
            fine_start(flow_ref, 3, slot)
            fine_inside()
            fine_wait(flow_ref, 3, slot)
            fine_edges(slot)
        return carry

    lax.fori_loop(0, CYCLES, cycle, 0)


def solution(mesh):
    GX, GY = mesh.shape["gx"], mesh.shape["gy"]

    def body(first_image, second_image, start_flow):
        NR, cols, depth = first_image.shape
        assert NR == 8 and cols == 8 and depth == 128 and GY % 8 == 0
        rounds = 1 + CYCLES * FINE_ROUNDS
        blocks = 1 + CYCLES * BLOCK_ROUNDS
        WR = 3 * NR // 2
        f32 = jnp.float32
        tile = (8, 128)
        vmem = lambda *front: pltpu.VMEM(front + tile, f32)
        return pl.pallas_call(
            functools.partial(kernel, GX, GY, NR),
            out_shape=jax.ShapeDtypeStruct(start_flow.shape, f32),
            in_specs=[pl.BlockSpec(memory_space=pltpu.VMEM)] * 3,
            out_specs=pl.BlockSpec(memory_space=pltpu.VMEM),
            scratch_shapes=[
                vmem(1, NR), vmem(1, NR), vmem(6, NR), vmem(3, NR), vmem(6, NR), vmem(6, NR),
                vmem(6, WR, 3), vmem(WR, 3), vmem(WR, 3), vmem(6, WR, 3), vmem(6, WR, 3), vmem(3, WR, 3),
                vmem(2, 3, WR, 3),
                vmem(6, GX, GY // 8), vmem(3, GX, GY // 8),
                pltpu.VMEM((3, GX + 4, GY + 16, 128), f32),
                vmem(rounds, 2, 3), vmem(rounds, 2, 3), vmem(rounds, 2, 3), vmem(rounds, 2, 3),
                vmem(blocks, 6), vmem(blocks, 8, 6),
                pltpu.VMEM((1 + CYCLES, 1, 128), f32),
                pltpu.VMEM((1 + CYCLES, GX * GY, 1, 128), f32),
                pltpu.SemaphoreType.DMA((rounds, 4)), pltpu.SemaphoreType.DMA((rounds, 4)),
                pltpu.SemaphoreType.DMA((blocks, 8)), pltpu.SemaphoreType.DMA((blocks, 8)),
                pltpu.SemaphoreType.DMA((1 + CYCLES,)), pltpu.SemaphoreType.DMA((1 + CYCLES,)),
            ],
            compiler_params=pltpu.CompilerParams(
                collective_id=0, has_side_effects=True, vmem_limit_bytes=48 * 1024 * 1024
            ),
            name="flow_cycles",
        )(first_image, second_image, start_flow)

    return jax.shard_map(
        body,
        mesh=mesh,
        in_specs=(P("gx", "gy", None), P("gx", "gy", None), P(None, "gx", "gy", None)),
        out_specs=P(None, "gx", "gy", None),
        check_vma=False,
    )
```

```python
import functools

import jax
import jax.numpy as jnp
from jax import lax
from jax.experimental import pallas as pl
from jax.experimental.pallas import tpu as pltpu
from jax.sharding import PartitionSpec as P

SWEEPS = 4
COARSE_SWEEPS = 12
CYCLES = 2
damping = 0.6
smooth_weight = 2.0
edge_scale = 0.25
floor_grad = 0.5
TINY = 1e-30

MESH = pl.DeviceIdType.MESH
SIDES = ((-1, 0), (1, 0), (0, -1), (0, 1))
AROUND = tuple((i, j) for i in (-1, 0, 1) for j in (-1, 0, 1) if (i, j) != (0, 0))
FINE_ROUNDS = 2 + 2 * SWEEPS
BLOCK_ROUNDS = 4


def sym(m, v):
    return [
        m[0] * v[0] + m[1] * v[1] + m[2] * v[2],
        m[1] * v[0] + m[3] * v[1] + m[4] * v[2],
        m[2] * v[0] + m[4] * v[1] + m[5] * v[2],
    ]


def damped_inverse(t, total):
    a, b, c, d, e, f = t[0] + total, t[1], t[2], t[3] + total, t[4], t[5] + total
    cof = [
        d * f - e * e,
        c * e - b * f,
        b * e - c * d,
        a * f - c * c,
        b * c - a * e,
        a * d - b * b,
    ]
    det = a * cof[0] + b * cof[1] + c * cof[2]
    factor = damping / jnp.where(total > 0.0, det, 1.0)
    return [factor * value for value in cof]


def kernel(
    GX, GY, NR, first_ref, second_ref, start_ref, flow_ref,
    mean_ref, weight_ref, tensor_ref, source_ref, rest_ref, face_ref, inv_ref,
    mid_t, mid_w, mid_face, mid_inv, mid_src, err,
    coarse_inv, coarse_src, corr,
    xh, yh, xs, ys, bs, br, gs, gb,
    f_send, f_recv, b_send, b_recv, g_send, g_recv,
):
    gx = lax.axis_index("gx")
    gy = lax.axis_index("gy")
    me = gx * GY + gy
    n = GX * GY
    GT = GY // 8
    NM = NR // 2
    WR = 3 * NM
    shape = (8, 128)
    lane = lax.broadcasted_iota(jnp.int32, shape, 1)
    sub = lax.broadcasted_iota(jnp.int32, shape, 0)
    zero = jnp.zeros(shape, jnp.float32)

    def lroll(v, k):
        return pltpu.roll(v, k % 128, 1)

    def sroll(v, k):
        return pltpu.roll(v, k % 8, 0)

    def lane_bit(k):
        return (lane & k) == 0

    def sub_bit(k):
        return (sub & k) == 0

    def lane_pair(v, k):
        return v + jnp.where(lane_bit(k), lroll(v, -k), lroll(v, k))

    def sub_pair(v, k):
        return v + jnp.where(sub_bit(k), sroll(v, -k), sroll(v, k))

    def zup(v, k):
        return jnp.where(lane < 128 - k, lroll(v, -k), 0.0)

    def zdn(v, k):
        return jnp.where(lane >= k, lroll(v, k), 0.0)

    def y_shifts(tiles, k):
        count = len(tiles)
        ups = [sroll(v, -k) for v in tiles] + [zero]
        downs = [zero] + [sroll(v, k) for v in tiles]
        return (
            [jnp.where(sub < 8 - k, ups[j], ups[j + 1]) for j in range(count)],
            [jnp.where(sub >= k, downs[j + 1], downs[j]) for j in range(count)],
        )

    def here(dx, dy):
        conds = []
        if dx:
            conds.append((gx + dx >= 0) & (gx + dx < GX))
        if dy:
            conds.append((gy + dy >= 0) & (gy + dy < GY))
        return functools.reduce(lambda p, q: p & q, conds)

    for ref in (xh, yh, br, corr):
        flat = 1
        for extent in ref.shape[:-2]:
            flat *= extent
        ref[...] = jnp.zeros(ref.shape, jnp.float32)

    barrier = pltpu.get_barrier_semaphore()

    def greet(d, carry):
        other = lax.rem(me + d, n)
        pl.semaphore_signal(
            barrier, inc=1, device_id=(other // GY, lax.rem(other, GY)), device_id_type=MESH
        )
        return carry

    lax.fori_loop(1, n, greet, 0)
    pl.semaphore_wait(barrier, n - 1)

    def side_copy(ref, count, slot, k):
        dx, dy = SIDES[k]
        back = k ^ 1
        if dx:
            src = xs.at[slot, k, pl.ds(0, count)]
            dst = xh.at[slot, back, pl.ds(0, count)]
        else:
            src = ys.at[slot, k - 2, pl.ds(0, count)]
            dst = yh.at[slot, back - 2, pl.ds(0, count)]
        return pltpu.make_async_remote_copy(
            src_ref=src, dst_ref=dst,
            send_sem=f_send.at[slot, k], recv_sem=f_recv.at[slot, back],
            device_id=(gx + dx, gy + dy), device_id_type=MESH,
        )

    def side_arrival(ref, count, slot, k):
        dx, dy = SIDES[k]
        if dx:
            dst = xh.at[slot, k, pl.ds(0, count)]
        else:
            dst = yh.at[slot, k - 2, pl.ds(0, count)]
        return pltpu.make_async_remote_copy(
            src_ref=dst, dst_ref=dst,
            send_sem=f_send.at[slot, k], recv_sem=f_recv.at[slot, k],
            device_id=(gx + dx, gy + dy), device_id_type=MESH,
        )

    def fine_start(ref, count, slot):
        for c in range(count):
            ys[slot, 0, c] = ref[c, :, 0, :]
            ys[slot, 1, c] = ref[c, :, 7, :]
            xs[slot, 0, c] = ref[c, 0]
            xs[slot, 1, c] = ref[c, NR - 1]
        for k in (2, 3, 0, 1):
            @pl.when(here(*SIDES[k]))
            def _(k=k):
                side_copy(ref, count, slot, k).start()

    def fine_wait(ref, count, slot):
        for k in (0, 1, 2, 3):
            @pl.when(here(*SIDES[k]))
            def _(k=k):
                side_arrival(ref, count, slot, k).wait_recv()
                side_copy(ref, count, slot, k).wait_send()

    def block_copy(count, slot, k):
        dx, dy = AROUND[k]
        return pltpu.make_async_remote_copy(
            src_ref=bs.at[slot, pl.ds(0, count)],
            dst_ref=br.at[slot, 7 - k, pl.ds(0, count)],
            send_sem=b_send.at[slot, k], recv_sem=b_recv.at[slot, 7 - k],
            device_id=(gx + dx, gy + dy), device_id_type=MESH,
        )

    def block_arrival(count, slot, k):
        dx, dy = AROUND[k]
        dst = br.at[slot, k, pl.ds(0, count)]
        return pltpu.make_async_remote_copy(
            src_ref=dst, dst_ref=dst,
            send_sem=b_send.at[slot, k], recv_sem=b_recv.at[slot, k],
            device_id=(gx + dx, gy + dy), device_id_type=MESH,
        )

    def pack(rows):
        lower = jnp.where(lane_bit(1), rows[0], rows[1])
        upper = jnp.where(lane_bit(1), rows[2], rows[3])
        return jnp.where(sub_bit(1), lower, upper)

    def unpack(v):
        even = jnp.where(lane_bit(1), v, lroll(v, 1))
        odd = jnp.where(lane_bit(1), lroll(v, -1), v)

        def split(w):
            return (
                jnp.where(sub_bit(1), w, sroll(w, 1)),
                jnp.where(sub_bit(1), sroll(w, -1), w),
            )

        e, o = split(even), split(odd)
        return [e[0], o[0], e[1], o[1]]

    def block_start(fields, slot):
        for i, rows in enumerate(fields):
            bs[slot, i] = pack(rows)
        for k in range(8):
            @pl.when(here(*AROUND[k]))
            def _(k=k):
                block_copy(len(fields), slot, k).start()

    def block_wait(count, slot):
        for k in range(8):
            @pl.when(here(*AROUND[k]))
            def _(k=k):
                block_arrival(count, slot, k).wait_recv()
                block_copy(count, slot, k).wait_send()

    def block_spread(places, slot):
        for k, (dx, dy) in enumerate(AROUND):
            for i, place in enumerate(places):
                for r, v in enumerate(unpack(br[slot, k, i])):
                    place[NM * (dx + 1) + r, dy + 1] = v

    def keep_own(place, rows):
        for r, v in enumerate(rows):
            place[NM + r, 1] = v

    def gather_copy(slot, other):
        return pltpu.make_async_remote_copy(
            src_ref=gs.at[slot], dst_ref=gb.at[slot, me],
            send_sem=g_send.at[slot], recv_sem=g_recv.at[slot],
            device_id=(other // GY, lax.rem(other, GY)), device_id_type=MESH,
        )

    def gather_start(values, slot):
        row = zero
        for i, v in enumerate(values):
            row = jnp.where((lane & 7) == i, v, row)
        gs[slot] = row[0:1]
        gb[slot, me] = row[0:1]

        def send(d, carry):
            gather_copy(slot, lax.rem(me + d, n)).start()
            return carry

        lax.fori_loop(1, n, send, 0)

    def gather_wait(slot):
        whole = gb.at[slot, pl.ds(0, n - 1)]
        copy = pltpu.make_async_remote_copy(
            src_ref=whole, dst_ref=whole,
            send_sem=g_send.at[slot], recv_sem=g_recv.at[slot],
            device_id=(gx, gy), device_id_type=MESH,
        )
        copy.wait_recv()
        copy.wait_send()

    def gathered(slot, count, g, t):
        packed = gb[slot, pl.ds(g * GY + t * 8, 8), 0, :]
        result = []
        for i in range(count):
            v = jnp.where((lane & 7) == i, packed, 0.0)
            for k in (1, 2, 4):
                v = lane_pair(v, k)
            result.append(v)
        return result

    def restrict_fine(rows):
        result = []
        for m in range(NM):
            v = rows[2 * m] + rows[2 * m + 1]
            result.append(sub_pair(lane_pair(v, 1), 1) * 0.125)
        return result

    def restrict_mid(rows):
        v = functools.reduce(lambda p, q: p + q, rows)
        for k in (2, 4):
            v = lane_pair(v, k)
            v = sub_pair(v, k)
        return v * (1.0 / 64.0)

    def fine_rows(ref, c, slot):
        return [xh[slot, 0, c]] + [ref[c, x] for x in range(NR)] + [xh[slot, 1, c]]

    def fine_y(rows, c, slot, x):
        v = rows[x + 1]
        up = jnp.where(sub < 7, sroll(v, -1), yh[slot, 1, c, x:x + 1, :])
        down = jnp.where(sub >= 1, sroll(v, 1), yh[slot, 0, c, x:x + 1, :])
        return up, down

    for x in range(NR):
        mean_ref[0, x] = 0.5 * (first_ref[x] + second_ref[x])
        for c in range(3):
            flow_ref[c, x] = start_ref[c, x]
    fine_start(mean_ref, 1, 0)
    fine_start(flow_ref, 3, 1)
    fine_wait(mean_ref, 1, 0)
    rows = fine_rows(mean_ref, 0, 0)
    for x in range(NR):
        up, down = fine_y(rows, 0, 0, x)
        s0 = 0.5 * (rows[x + 2] - rows[x])
        s1 = 0.5 * (up - down)
        s2 = 0.5 * (zup(rows[x + 1], 1) - zdn(rows[x + 1], 1))
        change = second_ref[x] - first_ref[x]
        scale = 1.0 / (s0 * s0 + s1 * s1 + s2 * s2 + floor_grad)
        a0, a1, a2 = scale * s0, scale * s1, scale * s2
        for i, v in enumerate((a0 * s0, a0 * s1, a0 * s2, a1 * s1, a1 * s2, a2 * s2)):
            tensor_ref[i, x] = v
        for i, v in enumerate((a0, a1, a2)):
            source_ref[i, x] = -v * change
    mids, coarses = [], []
    for i in range(6):
        own = restrict_fine([tensor_ref[i, x] for x in range(NR)])
        keep_own(mid_t.at[i], own)
        mids.append(own)
        coarses.append(restrict_mid(own))
    block_start(mids, 0)
    gather_start(coarses, 0)
    cface = smooth_weight / 64.0

    def mid_arrives():
        block_wait(6, 0)
        block_spread([mid_t.at[i] for i in range(6)], 0)

    def coarse_arrives():
        gather_wait(0)
        for g in range(GX):
            coarse_row(g)

    def coarse_row(g):
        for t in range(GT):
            tensor = gathered(0, 6, g, t)
            count = jnp.where(lane < 120, 1.0, 0.0) + jnp.where(lane >= 8, 1.0, 0.0)
            count = count + jnp.where(sub + t * 8 < GY - 1, 1.0, 0.0)
            count = count + jnp.where(sub + t * 8 >= 1, 1.0, 0.0)
            count = count + float((g > 0) + (g < GX - 1))
            for i, v in enumerate(damped_inverse(tensor, cface * count)):
                coarse_inv[i, g, t] = v

    def fine_inflow(x, all_rows, slot):
        flows = []
        face = [face_ref[i, x] for i in range(6)]
        for c in range(3):
            rows = all_rows[c]
            up, down = fine_y(rows, c, slot, x)
            v = source_ref[c, x] + face[0] * rows[x + 2] + face[1] * rows[x]
            v = v + face[2] * up + face[3] * down
            v = v + face[4] * lroll(rows[x + 1], -1) + face[5] * lroll(rows[x + 1], 1)
            flows.append(v)
        return flows, face

    def fine_inside():
        rows = [[flow_ref[c, x] for x in range(NR)] for c in range(3)]
        for x in range(NR):
            flows = []
            for c in range(3):
                now = rows[c][x]
                v = source_ref[c, x] + face_ref[4, x] * lroll(now, -1)
                v = v + face_ref[5, x] * lroll(now, 1)
                v = v + face_ref[2, x] * jnp.where(sub < 7, sroll(now, -1), 0.0)
                v = v + face_ref[3, x] * jnp.where(sub >= 1, sroll(now, 1), 0.0)
                if x < NR - 1:
                    v = v + face_ref[0, x] * rows[c][x + 1]
                if x > 0:
                    v = v + face_ref[1, x] * rows[c][x - 1]
                flows.append(v)
            out = sym([inv_ref[i, x] for i in range(6)], flows)
            for c in range(3):
                flow_ref[c, x] = (1.0 - damping) * rows[c][x] + out[c]

    def fine_edges(slot):
        for side, x, face in ((0, 0, 1), (1, NR - 1, 0)):
            outer = [face_ref[face, x] * xh[slot, side, c] for c in range(3)]
            out = sym([inv_ref[i, x] for i in range(6)], outer)
            for c in range(3):
                flow_ref[c, x] = flow_ref[c, x] + out[c]
        for side, y, face in ((0, 0, 3), (1, 7, 2)):
            outer = [face_ref[face, :, y, :] * yh[slot, side, c] for c in range(3)]
            out = sym([inv_ref[i, :, y, :] for i in range(6)], outer)
            for c in range(3):
                flow_ref[c, :, y, :] = flow_ref[c, :, y, :] + out[c]

    def mid_inflow(r, p, tiles, wanted):
        flows = [[None] * 3 for _ in range(3)]
        for c in range(3):
            now = [err[p, c, r, j] for j in range(3)]
            tiles[c] = now
            ups, downs = y_shifts(now, 2)
            for j in wanted:
                v = mid_src[c, r, j] + mid_face[0, r, j] * err[p, c, r + 1, j]
                v = v + mid_face[1, r, j] * err[p, c, r - 1, j]
                v = v + mid_face[2, r, j] * ups[j] + mid_face[3, r, j] * downs[j]
                v = v + mid_face[4, r, j] * lroll(now[j], -2)
                flows[c][j] = v + mid_face[5, r, j] * lroll(now[j], 2)
        return flows

    def mid_relax(p, low):
        def turn(r, carry):
            r = low + 2 * r
            done = []
            for u in range(2):
                tiles = [None] * 3
                flows = mid_inflow(r + u, p, tiles, (0, 1, 2))
                for j in range(3):
                    matrix = [mid_inv[i, r + u, j] for i in range(6)]
                    out = sym(matrix, [flows[c][j] for c in range(3)])
                    for c in range(3):
                        done.append((c, u, j, (1.0 - damping) * tiles[c][j] + out[c]))
            for c, u, j, v in done:
                err[1 - p, c, r + u, j] = v
            return carry

        lax.fori_loop(0, (WR - 2 * low) // 2, turn, 0)

    def mid_prepare():
        scale = 2.0 * smooth_weight / 4.0

        def turn(r, carry):
            now = [mid_w[r, j] for j in range(3)]
            has_up = jnp.where(r < WR - 1, 1.0, 0.0)
            has_down = jnp.where(r > 0, 1.0, 0.0)
            above = jnp.minimum(r + 1, WR - 1)
            below = jnp.maximum(r - 1, 0)
            ups, downs = y_shifts(now, 2)
            for j in range(3):
                v = now[j]
                beside = [
                    mid_w[above, j] * has_up, mid_w[below, j] * has_down,
                    ups[j], downs[j], zup(v, 2), zdn(v, 2),
                ]
                face = [scale * v * o / jnp.maximum(v + o, TINY) for o in beside]
                total = functools.reduce(lambda p, q: p + q, face)
                for i in range(6):
                    mid_face[i, r, j] = face[i]
                tensor = [mid_t[i, r, j] for i in range(6)]
                for i, w in enumerate(damped_inverse(tensor, total)):
                    mid_inv[i, r, j] = w
            return carry

        lax.fori_loop(0, WR, turn, 0)

    def cycle(cyc, carry):
        base = 1 + cyc * FINE_ROUNDS
        bbase = 1 + cyc * BLOCK_ROUNDS

        @pl.when(cyc > 0)
        def _():
            fine_start(flow_ref, 3, base)

        fine_wait(flow_ref, 3, base)
        q = [zero] * NR
        for c in range(3):
            rows = fine_rows(flow_ref, c, base)
            for x in range(NR):
                up, down = fine_y(rows, c, base, x)
                s0 = 0.5 * (rows[x + 2] - rows[x])
                s1 = 0.5 * (up - down)
                s2 = 0.5 * (zup(rows[x + 1], 1) - zdn(rows[x + 1], 1))
                q[x] = q[x] + s0 * s0 + s1 * s1 + s2 * s2
        weights = [lax.rsqrt(1.0 + v * (1.0 / edge_scale)) for v in q]
        for x in range(NR):
            weight_ref[0, x] = weights[x]
        fine_start(weight_ref, 1, base + 1)
        own_w = restrict_fine(weights)
        keep_own(mid_w, own_w)
        block_start([own_w], bbase)
        fine_wait(weight_ref, 1, base + 1)
        rows = fine_rows(weight_ref, 0, base + 1)
        for x in range(NR):
            v = rows[x + 1]
            up, down = fine_y(rows, 0, base + 1, x)
            beside = [rows[x + 2], rows[x], up, down, zup(v, 1), zdn(v, 1)]
            face = [2.0 * smooth_weight * v * o / (v + o) for o in beside]
            total = functools.reduce(lambda p, q: p + q, face)
            for i in range(6):
                face_ref[i, x] = face[i]
            tensor = [tensor_ref[i, x] for i in range(6)]
            for i, w in enumerate(damped_inverse(tensor, total)):
                inv_ref[i, x] = w
        fine_inside()
        fine_edges(base)
        for sweep in range(1, SWEEPS):
            slot = base + 1 + sweep
            fine_start(flow_ref, 3, slot)
            fine_inside()
            if sweep == 1:
                block_wait(1, bbase)
                block_spread([mid_w], bbase)
                pl.when(cyc == 0)(mid_arrives)
            if sweep == 2:
                mid_prepare()
            if sweep == 3:
                pl.when(cyc == 0)(coarse_arrives)
            fine_wait(flow_ref, 3, slot)
            fine_edges(slot)
        slot = base + 1 + SWEEPS
        fine_start(flow_ref, 3, slot)
        now = [[flow_ref[c, x] for x in range(NR)] for c in range(3)]
        for x in range(NR):
            face = [face_ref[i, x] for i in range(6)]
            total = functools.reduce(lambda p, q: p + q, face)
            out = sym([tensor_ref[i, x] for i in range(6)], [now[c][x] for c in range(3)])
            for c in range(3):
                v = now[c][x]
                r = source_ref[c, x] - out[c] - total * v
                r = r + face[4] * lroll(v, -1) + face[5] * lroll(v, 1)
                r = r + face[2] * jnp.where(sub < 7, sroll(v, -1), 0.0)
                r = r + face[3] * jnp.where(sub >= 1, sroll(v, 1), 0.0)
                if x < NR - 1:
                    r = r + face[0] * now[c][x + 1]
                if x > 0:
                    r = r + face[1] * now[c][x - 1]
                rest_ref[c, x] = r
        fine_wait(flow_ref, 3, slot)
        for c in range(3):
            rest_ref[c, 0] = rest_ref[c, 0] + face_ref[1, 0] * xh[slot, 0, c]
            rest_ref[c, NR - 1] = rest_ref[c, NR - 1] + face_ref[0, NR - 1] * xh[slot, 1, c]
            for side, y, k in ((0, 0, 3), (1, 7, 2)):
                rest_ref[c, :, y, :] = rest_ref[c, :, y, :] + face_ref[k, :, y, :] * yh[slot, side, c]
        rest = [[rest_ref[c, x] for x in range(NR)] for c in range(3)]
        srcs = [restrict_fine(rest[c]) for c in range(3)]
        errs = [[], [], []]
        for r in range(NM):
            out = sym([mid_inv[i, NM + r, 1] for i in range(6)], [srcs[c][r] for c in range(3)])
            for c in range(3):
                errs[c].append(out[c])
        block_start(srcs + errs, bbase + 1)
        for c in range(3):
            keep_own(mid_src.at[c], srcs[c])
            keep_own(err.at[0, c], errs[c])
        block_wait(6, bbase + 1)
        block_spread([mid_src.at[c] for c in range(3)] + [err.at[0, c] for c in range(3)], bbase + 1)
        p = 0
        for sweep in range(1, SWEEPS):
            mid_relax(p, sweep)
            p = 1 - p
        mrest = [[], [], []]
        olds = [[], [], []]
        for r in range(NM, 2 * NM):
            tiles = [None] * 3
            flows = mid_inflow(r, p, tiles, (1,))
            total = functools.reduce(lambda a, b: a + b, [mid_face[i, r, 1] for i in range(6)])
            now = [tiles[c][1] for c in range(3)]
            out = sym([mid_t[i, r, 1] for i in range(6)], now)
            for c in range(3):
                mrest[c].append(flows[c][1] - out[c] - total * now[c])
                olds[c].append(now[c])
        gather_start([restrict_mid(mrest[c]) for c in range(3)], 1 + cyc)
        block_start(olds, bbase + 2)
        block_wait(3, bbase + 2)
        block_spread([err.at[p, c] for c in range(3)], bbase + 2)
        gather_wait(1 + cyc)

        current = []
        for g in range(GX):
            for t in range(GT):
                src = gathered(1 + cyc, 3, g, t)
                out = sym([coarse_inv[i, g, t] for i in range(6)], src)
                for c in range(3):
                    coarse_src[c, g, t] = src[c]
                current.append(out)

        def coarse_turn(index, now):
            result = []
            for g in range(GX):
                shifted = [
                    y_shifts([now[g * GT + t][c] for t in range(GT)], 1) for c in range(3)
                ]
                for t in range(GT):
                    flows = []
                    for c in range(3):
                        v = now[g * GT + t][c]
                        s = shifted[c][0][t] + shifted[c][1][t]
                        s = s + (zup(v, 8) + zdn(v, 8))
                        if g > 0:
                            s = s + now[(g - 1) * GT + t][c]
                        if g < GX - 1:
                            s = s + now[(g + 1) * GT + t][c]
                        flows.append(coarse_src[c, g, t] + cface * s)
                    out = sym([coarse_inv[i, g, t] for i in range(6)], flows)
                    result.append(
                        [(1.0 - damping) * now[g * GT + t][c] + out[c] for c in range(3)]
                    )
            return result

        current = lax.fori_loop(0, COARSE_SWEEPS - 1, coarse_turn, current)
        ratio = NM
        step = (lane // 2) & 3
        lane_far = jnp.where((step == 0) | (step == 3), 0.375, 0.125)
        sub_far = jnp.where(((sub // 2) == 0) | ((sub // 2) == 3), 0.375, 0.125)
        for g in range(GX):
            for t in range(GT):
                for c in range(3):
                    v = current[g * GT + t][c]
                    other = jnp.where(step < 2, zdn(v, 8), zup(v, 8))
                    corr[c, 2 + g, 8 + 8 * t:16 + 8 * t, :] = (1.0 - lane_far) * v + lane_far * other
        for c in range(3):
            columns = []
            for i in range(5):
                cells = [
                    jnp.broadcast_to(corr[c, gx + i, pl.ds(gy + 6 + j, 1), :], shape)
                    for j in range(5)
                ]
                columns.append([
                    (1.0 - sub_far) * cells[j] + sub_far * jnp.where(sub < 4, cells[j - 1], cells[j + 1])
                    for j in (1, 2, 3)
                ])
            for r in range(WR):
                b, d = r // ratio + 1, r % ratio
                shift = (d + 0.5) / ratio - 0.5
                o = b - 1 if shift < 0 else b + 1
                for j in range(3):
                    lifted = (1.0 - abs(shift)) * columns[b][j] + abs(shift) * columns[o][j]
                    err[p, c, r, j] = err[p, c, r, j] + lifted
        for sweep in range(1, SWEEPS + 1):
            mid_relax(p, sweep)
            p = 1 - p
        block_start(
            [[err[p, c, NM + r, 1] for r in range(NM)] for c in range(3)], bbase + 3
        )
        block_wait(3, bbase + 3)
        block_spread([err.at[p, c] for c in range(3)], bbase + 3)
        for c in range(3):
            raised = []
            for r in range(NM - 1, 2 * NM + 1):
                tiles = [err[p, c, r, j] for j in range(3)]
                ups, downs = y_shifts(tiles, 2)
                v = 0.75 * tiles[1] + 0.25 * jnp.where(sub_bit(1), downs[1], ups[1])
                v = 0.75 * v + 0.25 * jnp.where(lane_bit(1), zdn(v, 2), zup(v, 2))
                raised.append(v)
            for x in range(NR):
                m = x // 2 + 1
                o = m - 1 if x % 2 == 0 else m + 1
                flow_ref[c, x] = flow_ref[c, x] + 0.75 * raised[m] + 0.25 * raised[o]
        for sweep in range(SWEEPS):
            slot = base + 2 + SWEEPS + sweep
            fine_start(flow_ref, 3, slot)
            fine_inside()
            fine_wait(flow_ref, 3, slot)
            fine_edges(slot)
        return carry

    lax.fori_loop(0, CYCLES, cycle, 0)


def solution(mesh):
    GX, GY = mesh.shape["gx"], mesh.shape["gy"]

    def body(first_image, second_image, start_flow):
        NR, cols, depth = first_image.shape
        assert NR == 8 and cols == 8 and depth == 128 and GY % 8 == 0
        rounds = 1 + CYCLES * FINE_ROUNDS
        blocks = 1 + CYCLES * BLOCK_ROUNDS
        WR = 3 * NR // 2
        f32 = jnp.float32
        tile = (8, 128)
        vmem = lambda *front: pltpu.VMEM(front + tile, f32)
        return pl.pallas_call(
            functools.partial(kernel, GX, GY, NR),
            out_shape=jax.ShapeDtypeStruct(start_flow.shape, f32),
            in_specs=[pl.BlockSpec(memory_space=pltpu.VMEM)] * 3,
            out_specs=pl.BlockSpec(memory_space=pltpu.VMEM),
            scratch_shapes=[
                vmem(1, NR), vmem(1, NR), vmem(6, NR), vmem(3, NR), vmem(3, NR), vmem(6, NR), vmem(6, NR),
                vmem(6, WR, 3), vmem(WR, 3), vmem(6, WR, 3), vmem(6, WR, 3), vmem(3, WR, 3),
                vmem(2, 3, WR, 3),
                vmem(6, GX, GY // 8), vmem(3, GX, GY // 8),
                pltpu.VMEM((3, GX + 4, GY + 16, 128), f32),
                vmem(rounds, 2, 3), vmem(rounds, 2, 3), vmem(rounds, 2, 3), vmem(rounds, 2, 3),
                vmem(blocks, 6), vmem(blocks, 8, 6),
                pltpu.VMEM((1 + CYCLES, 1, 128), f32),
                pltpu.VMEM((1 + CYCLES, GX * GY, 1, 128), f32),
                pltpu.SemaphoreType.DMA((rounds, 4)), pltpu.SemaphoreType.DMA((rounds, 4)),
                pltpu.SemaphoreType.DMA((blocks, 8)), pltpu.SemaphoreType.DMA((blocks, 8)),
                pltpu.SemaphoreType.DMA((1 + CYCLES,)), pltpu.SemaphoreType.DMA((1 + CYCLES,)),
            ],
            compiler_params=pltpu.CompilerParams(
                collective_id=0, has_side_effects=True, vmem_limit_bytes=48 * 1024 * 1024
            ),
            name="flow_cycles",
        )(first_image, second_image, start_flow)

    return jax.shard_map(
        body,
        mesh=mesh,
        in_specs=(P("gx", "gy", None), P("gx", "gy", None), P(None, "gx", "gy", None)),
        out_specs=P(None, "gx", "gy", None),
        check_vma=False,
    )
```
